256 devices in a mesh: space: 8 (over z), tm: 16 (over y, x), param: 2 (over core).
Axes of the slice: x: 4, y: 4, z: 8, core: 2. Of those that a mesh axis runs over, the one named last changes fastest.
Arguments:
- snapshots: float32 [512, 64, 6144], P('tm', 'param', 'space'), may hold values from -6 to 6
- time_basis: float32 [512, 64], replicated, may hold values from -0.25 to 0.25
Outputs:
- gram_time: float32 [512, 512], P('tm')
- core: float32 [64, 64, 6144], P('tm', 'param', 'space')
- gram_param: float32 [64, 64], P('param')
The draws below stay inside these ranges and needn't reach their ends.
All inputs are finite; a program needn't handle non-finite values.
Results may differ from the reference program's by a relative error of at most 0.000071.
Values sent between devices are 32-bit elements; how exact they have to be, the bound alone decides.
A program may use at most 128 MiB of HBM per device.

```python
import jax
import jax.numpy as jnp
from jax import lax

TT = 512
RANK = 64
LOADS = 64
POINTS = 6144


def block_scale(own_key, shape, cuts, least, top_value):
    def one(dim, blocks):
        steps = jax.random.uniform(jax.random.fold_in(jax.random.fold_in(own_key, 6), dim), (blocks,), jnp.float32, least / len(cuts), top_value / len(cuts))
        return jnp.repeat(jnp.exp(steps), shape[dim] // blocks).reshape((-1,) + (1,) * (len(shape) - dim - 1))

    loudness = one(*cuts[0])
    for cut in cuts[1:]:
        loudness = loudness * one(*cut)
    return loudness


def gaussian(own_key, extent, spread, limit, pieces=(), held_as=jnp.bfloat16):
    values = spread * jax.random.normal(own_key, extent, jnp.float32)
    if pieces:
        values = values * block_scale(own_key, extent, pieces, -0.22, 0.18)
    return jnp.clip(values, -limit, limit).astype(held_as)


def setup_inputs(seed: int = 0) -> dict:
    streams_of = jax.random.split(jax.random.key(seed), 3)
    snapshots = gaussian(streams_of[0], (TT, LOADS, POINTS), 1.0, 6.0, ((0, 16), (1, 2), (2, 8)), jnp.float32)
    time_basis = gaussian(streams_of[1], (TT, RANK), TT ** -0.5, 0.25, (), jnp.float32)
    return {"snapshots": snapshots, "time_basis": time_basis}


def reference(snapshots, time_basis):
    flat = snapshots.reshape(TT, LOADS * POINTS)
    gram_time = jnp.dot(flat, flat.T, precision=lax.Precision.HIGHEST, preferred_element_type=jnp.float32) / (LOADS * POINTS)
    core_flat = jnp.dot(time_basis.T, flat, precision=lax.Precision.HIGHEST, preferred_element_type=jnp.float32)
    core = core_flat.reshape(RANK, LOADS, POINTS)
    gram_param = jnp.einsum("rps,rqs->pq", core, core, precision=lax.Precision.HIGHEST) / (RANK * POINTS)
    return gram_time, core, gram_param
```

```python
import functools

import jax
import jax.numpy as jnp
from jax import lax
from jax.experimental import pallas as pl
from jax.experimental.pallas import tpu as pltpu
from jax.sharding import PartitionSpec as P

MESH = pl.DeviceIdType.MESH
NT = (((1,), (1,)), ((), ()))
NN = (((1,), (0,)), ((), ()))
LANE = 128
ORDER = (
    (1, 0), (0, 1), (3, 0), (0, 3), (1, 1), (3, 3), (1, 3), (3, 1),
    (2, 0), (0, 2), (2, 1), (1, 2), (2, 3), (3, 2), (2, 2),
)


def dot(a, b, dims):
    return lax.dot_general(a, b, dims, preferred_element_type=jnp.float32)


def split(v):
    high = v.astype(jnp.bfloat16)
    return high, (v - high.astype(jnp.float32)).astype(jnp.bfloat16)


def kernel(
    scale_time, scale_param,
    x_hbm, basis_ref, time_out, core_out, param_out,
    staged, sent, held, high_buf, low_buf, basis_high, basis_low,
    gram, gram_sib, gram_sum, gram_rows, tile_in, tile_mine, tiles,
    core_sent, core_held, core_sib, rank_high, rank_low,
    part_mine, part_in, part_sum, part_z,
    load_sem, x_send, x_recv, c_send, c_recv, cs_sem, cs_rsem,
    gs_send, gs_recv, gr_send, gr_recv, gz_send, gz_recv, ga_send, ga_recv,
    px_send, px_recv, pz_send, pz_recv,
):
    sp, tm, me = lax.axis_index("space"), lax.axis_index("tm"), lax.axis_index("param")
    y, x = tm // 4, lax.rem(tm, 4)
    chunks = staged.shape[0]
    steps = staged.shape[1]

    def peer(dx, dy):
        return lax.rem(y + dy, 4) * 4 + lax.rem(x + dx, 4)

    def along(dz):
        return lax.rem(sp + dz, 8)

    def remote(src, dst, ssem, rsem, target):
        return pltpu.make_async_remote_copy(
            src_ref=src, dst_ref=dst, send_sem=ssem, recv_sem=rsem,
            device_id=target, device_id_type=MESH,
        )

    sibling = (sp, tm, 1 - me)

    for k in range(chunks):
        pltpu.make_async_copy(
            x_hbm.at[:, :, pl.ds(k * LANE, LANE)], staged.at[k], load_sem.at[k]
        ).start()

    barrier = pltpu.get_barrier_semaphore()
    for dx, dy in ORDER:
        pl.semaphore_signal(barrier, inc=1, device_id=(sp, peer(dx, dy), me), device_id_type=MESH)
    for dz in range(8):
        if dz:
            pl.semaphore_signal(barrier, inc=1, device_id=(along(dz), tm, me), device_id_type=MESH)
        pl.semaphore_signal(barrier, inc=1, device_id=(along(dz), tm, 1 - me), device_id_type=MESH)

    for k in range(chunks):
        pltpu.make_async_copy(
            x_hbm.at[:, :, pl.ds(k * LANE, LANE)], staged.at[k], load_sem.at[k]
        ).wait()
        flat = staged.at[k].reshape(steps * steps, LANE)
        for j in range(16):
            for pp in range(2):
                sent[k, j, pp] = flat[pl.ds(2 * j + pp, steps, stride=steps), :]
        held[k, tm] = sent[k, tm]
        if k == 0:
            pl.semaphore_wait(barrier, 30)
        for dx, dy in ORDER:
            to = peer(dx, dy)
            remote(
                sent.at[k, to], held.at[k, tm], x_send, x_recv.at[k], (sp, to, me)
            ).start()

    row = lax.broadcasted_iota(jnp.int32, (128, 64), 0)
    col = lax.broadcasted_iota(jnp.int32, (128, 64), 1)
    parts = split(basis_ref[...])
    for pp in range(2):
        pick = jnp.where(
            (lax.rem(row, 8) // 4 == pp) & (col == (row // 8) * 4 + lax.rem(row, 4)), 1.0, 0.0
        ).astype(jnp.bfloat16)
        basis_high[pp] = dot(pick, parts[0], NT).astype(jnp.bfloat16)
        basis_low[pp] = dot(pick, parts[1], NT).astype(jnp.bfloat16)

    gram[...] = jnp.zeros_like(gram)

    for k in range(chunks):
        remote(
            sent.at[k, pl.ds(0, 15)], held.at[k, pl.ds(0, 15)], x_send, x_recv.at[k], sibling
        ).wait_recv()
        for pp in range(2):
            high, low = split(held[k, :, pp].reshape(512, LANE))
            high_buf[:, pp * LANE:(pp + 1) * LANE] = high
            low_buf[:, pp * LANE:(pp + 1) * LANE] = low
        total = None
        for pp in range(2):
            high = high_buf[:, pp * LANE:(pp + 1) * LANE]
            low = low_buf[:, pp * LANE:(pp + 1) * LANE]
            term = (
                dot(basis_high[pp], low, NN) + dot(basis_low[pp], high, NN)
            ) + dot(basis_high[pp], high, NN)
            total = term if total is None else total + term
        core_sent[k] = total.reshape(16, 8, LANE)
        core_held[k, tm] = core_sent[k, tm]
        for dx, dy in ORDER:
            to = peer(dx, dy)
            remote(
                core_sent.at[k, to], core_held.at[k, tm], c_send, c_recv, (sp, to, me)
            ).start()
        for dy in range(4):
            there = lax.rem(y + dy, 4)
            rows = pl.ds(pl.multiple_of(there * 128, 128), 128)
            high, low = high_buf[rows, :], low_buf[rows, :]
            add = (
                dot(high, low_buf[...], NT) + dot(low, high_buf[...], NT)
            ) + dot(high, high_buf[...], NT)
            blocks = pl.ds(there * 4, 4)
            gram[blocks] = gram[blocks] + add.reshape(4, 2, 16, 512)
            if k == chunks - 1:
                remote(
                    gram.at[blocks, 1 - me], gram_sib.at[blocks],
                    gs_send.at[dy], gs_recv.at[dy], sibling,
                ).start()

    for dy in range(4):
        blocks = pl.ds(lax.rem(y + dy, 4) * 4, 4)
        remote(
            gram.at[blocks, 1 - me], gram_sib.at[blocks],
            gs_send.at[dy], gs_recv.at[dy], sibling,
        ).wait_recv()
        gram_sum[blocks] = gram[blocks, me] + gram_sib[blocks]
        for dx in range(4):
            to = peer(dx, dy)
            if dx == 0 and dy == 0:
                gram_rows[tm] = gram_sum[tm]
            else:
                remote(
                    gram_sum.at[to], gram_rows.at[tm], gr_send, gr_recv, (sp, to, me)
                ).start()

    remote(
        sent.at[0, pl.ds(0, 15)], core_held.at[:, pl.ds(0, 15)], c_send, c_recv, sibling
    ).wait_recv()
    swap = remote(core_held, core_sib, cs_sem, cs_rsem, sibling)
    swap.start()
    for k in range(chunks):
        flat = core_held.at[k].reshape(128, LANE)
        for r in range(4):
            v = flat[pl.ds(r, 32, stride=4), :]
            core_out[r, :, k * LANE:(k + 1) * LANE] = v
            high, low = split(v)
            rank_high[me, r, :, k * LANE:(k + 1) * LANE] = high
            rank_low[me, r, :, k * LANE:(k + 1) * LANE] = low
    swap.wait_recv()
    for k in range(chunks):
        flat = core_sib.at[k].reshape(128, LANE)
        for r in range(4):
            high, low = split(flat[pl.ds(r, 32, stride=4), :])
            rank_high[1 - me, r, :, k * LANE:(k + 1) * LANE] = high
            rank_low[1 - me, r, :, k * LANE:(k + 1) * LANE] = low
    part = jnp.zeros((32, 64), jnp.float32)
    for r in range(4):
        high, low = rank_high[me, r], rank_low[me, r]
        all_high = rank_high[:, r].reshape(64, high.shape[1])
        all_low = rank_low[:, r].reshape(64, high.shape[1])
        part = part + (
            (dot(high, all_low, NT) + dot(low, all_high, NT)) + dot(high, all_high, NT)
        )
    part_mine[...] = jnp.concatenate([part[:16], part[16:]], axis=1)
    part_in[tm] = part_mine[...]
    for dx, dy in ORDER:
        remote(
            part_mine, part_in.at[tm], px_send, px_recv, (sp, peer(dx, dy), me)
        ).start()

    remote(
        gram_sum.at[pl.ds(0, 15)], gram_rows.at[pl.ds(0, 15)], gr_send, gr_recv, sibling
    ).wait_recv()
    rows = gram_rows[0]
    for j in range(1, 16):
        rows = rows + gram_rows[j]
    for q in range(8):
        tile_mine[q] = rows[(q // 4) * 8:(q // 4) * 8 + 8, (q % 4) * LANE:(q % 4 + 1) * LANE]
    tile_in[sp] = tile_mine[sp]
    for dz in (1, 7, 2, 6, 3, 5, 4):
        to = along(dz)
        remote(tile_mine.at[to], tile_in.at[sp], gz_send, gz_recv, (to, tm, me)).start()

    remote(
        part_in.at[pl.ds(0, 15)], part_in.at[pl.ds(0, 15)], px_send, px_recv, sibling
    ).wait_recv()
    part = part_in[0]
    for j in range(1, 16):
        part = part + part_in[j]
    part_sum[...] = part
    part_z[sp] = part
    for dz in (1, 7, 2, 6, 3, 5, 4):
        to = along(dz)
        remote(part_sum, part_z.at[sp], pz_send, pz_recv, (to, tm, me)).start()

    remote(
        tile_mine.at[pl.ds(0, 7)], tile_in.at[pl.ds(0, 7)], gz_send, gz_recv, sibling
    ).wait_recv()
    tile = tile_in[0]
    for j in range(1, 8):
        tile = tile + tile_in[j]
    slot = me * 8 + sp
    tiles[slot] = tile * scale_time
    for dz in (0, 1, 7, 2, 6, 3, 5, 4):
        to = along(dz)
        if dz:
            remote(tiles.at[slot], tiles.at[slot], ga_send, ga_recv, (to, tm, me)).start()
        remote(tiles.at[slot], tiles.at[slot], ga_send, ga_recv, (to, tm, 1 - me)).start()

    remote(
        part_z.at[pl.ds(0, 7)], part_z.at[pl.ds(0, 7)], pz_send, pz_recv, sibling
    ).wait_recv()
    part = part_z[0]
    for j in range(1, 8):
        part = part + part_z[j]
    part = part * scale_param
    param_out[0:16, :] = part[:, :64]
    param_out[16:32, :] = part[:, 64:]

    remote(
        tiles.at[pl.ds(0, 15)], tiles.at[pl.ds(0, 15)], ga_send, ga_recv, sibling
    ).wait_recv()
    for q in range(16):
        time_out[(q // 4) * 8:(q // 4) * 8 + 8, (q % 4) * LANE:(q % 4 + 1) * LANE] = tiles[q]

    remote(
        sent.at[:, pl.ds(0, 15)], held.at[:, pl.ds(0, 15)], x_send, x_recv.at[0], sibling
    ).wait_send()
    remote(
        core_sent.at[:, pl.ds(0, 15)], core_held.at[:, pl.ds(0, 15)], c_send, c_recv, sibling
    ).wait_send()
    for dy in range(4):
        blocks = pl.ds(lax.rem(y + dy, 4) * 4, 4)
        remote(
            gram.at[blocks, 1 - me], gram_sib.at[blocks],
            gs_send.at[dy], gs_recv.at[dy], sibling,
        ).wait_send()
    swap.wait_send()
    remote(
        gram_sum.at[pl.ds(0, 15)], gram_rows.at[pl.ds(0, 15)], gr_send, gr_recv, sibling
    ).wait_send()
    remote(
        part_in.at[pl.ds(0, 15)], part_in.at[pl.ds(0, 15)], px_send, px_recv, sibling
    ).wait_send()
    remote(
        tile_mine.at[pl.ds(0, 7)], tile_in.at[pl.ds(0, 7)], gz_send, gz_recv, sibling
    ).wait_send()
    remote(
        part_z.at[pl.ds(0, 7)], part_z.at[pl.ds(0, 7)], pz_send, pz_recv, sibling
    ).wait_send()
    remote(
        tiles.at[pl.ds(0, 15)], tiles.at[pl.ds(0, 15)], ga_send, ga_recv, sibling
    ).wait_send()


def body(snapshots, time_basis):
    f32, bf16 = jnp.float32, jnp.bfloat16
    time_local, load_local, point_local = snapshots.shape
    columns = load_local * 2 * point_local * 8
    rank = time_basis.shape[1]
    k = point_local // LANE
    vmem = pltpu.VMEM
    dma = pltpu.SemaphoreType.DMA
    return pl.pallas_call(
        functools.partial(kernel, 1.0 / columns, 1.0 / (rank * point_local * 8)),
        out_shape=(
            jax.ShapeDtypeStruct((32, 512), f32),
            jax.ShapeDtypeStruct((4, 32, point_local), f32),
            jax.ShapeDtypeStruct((32, 64), f32),
        ),
        in_specs=[pl.BlockSpec(memory_space=pl.ANY), pl.BlockSpec(memory_space=vmem)],
        out_specs=(pl.BlockSpec(memory_space=vmem),) * 3,
        scratch_shapes=[
            vmem((k, time_local, load_local, LANE), f32),
            vmem((k, 16, 2, time_local, LANE), f32),
            vmem((k, 16, 2, time_local, LANE), f32),
            vmem((512, 2 * LANE), bf16),
            vmem((512, 2 * LANE), bf16),
            vmem((2, 128, 512), bf16),
            vmem((2, 128, 512), bf16),
            vmem((16, 2, 16, 512), f32),
            vmem((16, 16, 512), f32),
            vmem((16, 16, 512), f32),
            vmem((16, 16, 512), f32),
            vmem((8, 8, LANE), f32),
            vmem((8, 8, LANE), f32),
            vmem((16, 8, LANE), f32),
            vmem((k, 16, 8, LANE), f32),
            vmem((k, 16, 8, LANE), f32),
            vmem((k, 16, 8, LANE), f32),
            vmem((2, 4, 32, point_local), bf16),
            vmem((2, 4, 32, point_local), bf16),
            vmem((16, LANE), f32),
            vmem((16, 16, LANE), f32),
            vmem((16, LANE), f32),
            vmem((8, 16, LANE), f32),
            dma((k,)), dma, dma((k,)), dma, dma, dma, dma,
            dma((4,)), dma((4,)), dma, dma, dma, dma, dma, dma,
            dma, dma, dma, dma,
        ],
        compiler_params=pltpu.CompilerParams(
            collective_id=0, has_side_effects=True, vmem_limit_bytes=56 * 1024 * 1024
        ),
    )(snapshots, time_basis)


def solution(mesh):
    return jax.shard_map(
        body,
        mesh=mesh,
        in_specs=(P("tm", "param", "space"), P()),
        out_specs=(P("tm", None), P("tm", "param", "space"), P("param", None)),
        check_vma=False,
    )
```

```python
import functools

import jax
import jax.numpy as jnp
from jax import lax
from jax.experimental import pallas as pl
from jax.experimental.pallas import tpu as pltpu
from jax.sharding import PartitionSpec as P

MESH = pl.DeviceIdType.MESH
NT = (((1,), (1,)), ((), ()))
NN = (((1,), (0,)), ((), ()))
LANE = 128
ORDER = (
    (1, 0), (0, 1), (3, 0), (0, 3), (1, 1), (3, 3), (1, 3), (3, 1),
    (2, 0), (0, 2), (2, 1), (1, 2), (2, 3), (3, 2), (2, 2),
)


def dot(a, b, dims):
    return lax.dot_general(a, b, dims, preferred_element_type=jnp.float32)


def split(v):
    high = v.astype(jnp.bfloat16)
    return high, (v - high.astype(jnp.float32)).astype(jnp.bfloat16)


def split_3(v):
    high = v.astype(jnp.bfloat16)
    rest = v - high.astype(jnp.float32)
    return (high,) + split(rest)


def kernel(
    scale_time, scale_param,
    x_hbm, basis_ref, time_out, core_out, param_out,
    staged, sent, mid, held, high_buf, low_buf, basis_high, basis_low,
    gram, gram_sib, gram_sum, gram_in, rows_mine, rows_in, tiles,
    core_sent, core_held, core_sib, pair_gram, pair_kept,
    part_mine, part_in, part_sum, part_z,
    load_sem, x1_send, x1_recv, x2_send, x2_recv, c_send, c_recv, cs_send, cs_recv,
    gs_send, gs_recv, g1_send, g1_recv, gz_send, gz_recv, gy_send, gy_recv,
    px_send, px_recv, pz_send, pz_recv,
):
    sp, tm, me = lax.axis_index("space"), lax.axis_index("tm"), lax.axis_index("param")
    y, x = tm // 4, lax.rem(tm, 4)
    chunks, steps = staged.shape[0], staged.shape[1]

    def peer(dx, dy):
        return lax.rem(y + dy, 4) * 4 + lax.rem(x + dx, 4)

    def along(dz):
        return lax.rem(sp + dz, 8)

    def remote(src, dst, ssem, rsem, target):
        return pltpu.make_async_remote_copy(
            src_ref=src, dst_ref=dst, send_sem=ssem, recv_sem=rsem,
            device_id=target, device_id_type=MESH,
        )

    sibling = (sp, tm, 1 - me)
    ring = (1, 3, 2)
    far = (4, 3, 5, 2, 6, 1, 7)

    def load(k):
        return pltpu.make_async_copy(
            x_hbm.at[:, :, pl.ds(k * LANE, LANE)], staged.at[k], load_sem.at[k]
        )

    for k in range(chunks):
        load(k).start()

    barrier = pltpu.get_barrier_semaphore()
    for dz in far:
        pl.semaphore_signal(barrier, inc=1, device_id=(along(dz), tm, me), device_id_type=MESH)
    for dx, dy in ORDER[::-1]:
        pl.semaphore_signal(barrier, inc=1, device_id=(sp, peer(dx, dy), me), device_id_type=MESH)
    pl.semaphore_signal(barrier, inc=1, device_id=sibling, device_id_type=MESH)

    for k in range(chunks):
        load(k).wait()
        flat = staged.at[k].reshape(steps * steps, LANE)
        for j in range(16):
            for pp in range(2):
                sent[k, pp, j // 4, j % 4] = flat[pl.ds(2 * j + pp, steps, stride=steps), :]
        if k == 0:
            pl.semaphore_wait(barrier, 23)
        for d in ring:
            tx, ty = lax.rem(x + d, 4), lax.rem(y + d, 4)
            remote(
                sent.at[k, 0, :, tx], mid.at[k, 0, x], x1_send, x1_recv.at[k, 0],
                (sp, y * 4 + tx, me),
            ).start()
            remote(
                sent.at[k, 1, ty], mid.at[k, 1, y], x1_send, x1_recv.at[k, 1],
                (sp, ty * 4 + x, me),
            ).start()
        mid[k, 0, x] = sent[k, 0, :, x]
        mid[k, 1, y] = sent[k, 1, y]

    row = lax.broadcasted_iota(jnp.int32, (128, 64), 0)
    col = lax.broadcasted_iota(jnp.int32, (128, 64), 1)
    parts = split(basis_ref[...])
    for pp in range(2):
        pick = jnp.where(
            (lax.rem(row, 8) // 4 == pp) & (col == (row // 8) * 4 + lax.rem(row, 4)), 1.0, 0.0
        ).astype(jnp.bfloat16)
        basis_high[pp] = dot(pick, parts[0], NN).astype(jnp.bfloat16)
        basis_low[pp] = dot(pick, parts[1], NN).astype(jnp.bfloat16)

    gram[...] = jnp.zeros_like(gram)
    pair_gram[...] = jnp.zeros_like(pair_gram)

    for k in range(chunks):
        for pp in range(2):
            remote(
                sent.at[k, pp, pl.ds(0, 3)], mid.at[k, pp, pl.ds(0, 3)],
                x1_send, x1_recv.at[k, pp], sibling,
            ).wait_recv()
        for d in ring:
            tx, ty = lax.rem(x + d, 4), lax.rem(y + d, 4)
            remote(
                mid.at[k, 0, :, ty], held.at[k, 0, y], x2_send, x2_recv.at[k],
                (sp, ty * 4 + x, me),
            ).start()
            remote(
                mid.at[k, 1, :, tx], held.at[k, 1, :, x], x2_send, x2_recv.at[k],
                (sp, y * 4 + tx, me),
            ).start()
        held[k, 0, y] = mid[k, 0, :, y]
        held[k, 1, :, x] = mid[k, 1, :, x]

    def core_back(k):
        remote(
            core_sent.at[k, pl.ds(0, 15)], core_held.at[k, pl.ds(0, 15)],
            c_send, c_recv.at[k], sibling,
        ).wait_recv()
        remote(
            core_held.at[k], core_sib.at[k], cs_send.at[k], cs_recv.at[k], sibling
        ).start()

    def core_write(k):
        flat = core_held.at[k].reshape(128, LANE)
        for r in range(4):
            core_out[r, :, k * LANE:(k + 1) * LANE] = flat[pl.ds(r, 32, stride=4), :]

    def core_pair(k):
        remote(
            core_held.at[k], core_sib.at[k], cs_send.at[k], cs_recv.at[k], sibling
        ).wait_recv()
        high, low = split(core_held[k].reshape(128, LANE))
        high_2, low_2 = split(core_sib[k].reshape(128, LANE))
        pair_gram[0] += (dot(high, low, NT) + dot(low, high, NT)) + dot(high, high, NT)
        pair_gram[1] += (dot(high, low_2, NT) + dot(low, high_2, NT)) + dot(high, high_2, NT)

    for k in range(chunks):
        remote(
            mid.at[k, :, pl.ds(0, 3)], held.at[k, :, pl.ds(0, 3)],
            x2_send, x2_recv.at[k], sibling,
        ).wait_recv()
        for pp in range(2):
            high, low = split(held[k, pp].reshape(512, LANE))
            high_buf[:, pp * LANE:(pp + 1) * LANE] = high
            low_buf[:, pp * LANE:(pp + 1) * LANE] = low
        total = None
        for pp in range(2):
            high = high_buf[:, pp * LANE:(pp + 1) * LANE]
            low = low_buf[:, pp * LANE:(pp + 1) * LANE]
            term = (
                dot(basis_high[pp], low, NN) + dot(basis_low[pp], high, NN)
            ) + dot(basis_high[pp], high, NN)
            total = term if total is None else total + term
        core_sent[k] = total.reshape(16, 8, LANE)
        core_held[k, tm] = core_sent[k, tm]
        for dx, dy in ORDER:
            to = peer(dx, dy)
            remote(
                core_sent.at[k, to], core_held.at[k, tm], c_send, c_recv.at[k], (sp, to, me)
            ).start()
        for dy in range(4):
            there = lax.rem(y + dy, 4)
            rows = pl.ds(pl.multiple_of(there * 128, 128), 128)
            high, low = high_buf[rows, :], low_buf[rows, :]
            add = (
                dot(high, low_buf[...], NT) + dot(low, high_buf[...], NT)
            ) + dot(high, high_buf[...], NT)
            blocks = pl.ds(there * 4, 4)
            gram[blocks] = gram[blocks] + add.reshape(4, 2, 16, 512)
            if k == chunks - 1:
                remote(
                    gram.at[blocks, 1 - me], gram_sib.at[blocks],
                    gs_send.at[dy], gs_recv.at[dy], sibling,
                ).start()

    for dy in range(4):
        there = lax.rem(y + dy, 4)
        blocks = pl.ds(there * 4, 4)
        remote(
            gram.at[blocks, 1 - me], gram_sib.at[blocks],
            gs_send.at[dy], gs_recv.at[dy], sibling,
        ).wait_recv()
        gram_sum[blocks] = gram[blocks, me] + gram_sib[blocks]
        for dx in (1, 3, 2, 0):
            to = peer(dx, dy)
            if dx or dy:
                remote(
                    gram_sum.at[to], gram_in.at[tm], g1_send, g1_recv, (sp, to, me)
                ).start()
    gram_in[tm] = gram_sum[tm]

    for k in range(chunks):
        core_back(k)
    for k in range(chunks):
        core_pair(k)
    row = lax.broadcasted_iota(jnp.int32, (128, 128), 0)
    col = lax.broadcasted_iota(jnp.int32, (128, 128), 1)
    same = lax.rem(row, 4) == lax.rem(col, 4)
    row = lax.broadcasted_iota(jnp.int32, (64, 128), 0)
    col = lax.broadcasted_iota(jnp.int32, (64, 128), 1)
    part = jnp.zeros((32, 64), jnp.float32)
    for other in range(2):
        at = (1 - me) if other else me
        place = jnp.where(row == at * 32 + col // 4, 1.0, 0.0).astype(jnp.bfloat16)
        pair_kept[...] = jnp.where(same, pair_gram[other], 0.0)
        summed = (
            (pair_kept[pl.ds(0, 32, stride=4), :] + pair_kept[pl.ds(1, 32, stride=4), :])
            + (pair_kept[pl.ds(2, 32, stride=4), :] + pair_kept[pl.ds(3, 32, stride=4), :])
        )
        for small in split_3(summed):
            part = part + dot(small, place, NT)
    part_mine[...] = jnp.concatenate([part[:16], part[16:]], axis=1)
    for dx, dy in ORDER[::-1]:
        remote(
            part_mine, part_in.at[tm], px_send, px_recv, (sp, peer(dx, dy), me)
        ).start()
    part_in[tm] = part_mine[...]

    remote(
        gram_sum.at[pl.ds(0, 15)], gram_in.at[pl.ds(0, 15)], g1_send, g1_recv, sibling
    ).wait_recv()
    rows = gram_in[0]
    for j in range(1, 16):
        rows = rows + gram_in[j]
    rows_mine[...] = rows
    for dz in far:
        remote(
            rows_mine, rows_in.at[sp], gz_send, gz_recv, (along(dz), tm, me)
        ).start()
    rows_in[sp] = rows

    remote(
        part_in.at[pl.ds(0, 15)], part_in.at[pl.ds(0, 15)], px_send, px_recv, sibling
    ).wait_recv()
    part = part_in[0]
    for j in range(1, 16):
        part = part + part_in[j]
    part_sum[...] = part
    for dz in far:
        to = along(dz)
        remote(part_sum, part_z.at[sp], pz_send, pz_recv, (to, tm, me)).start()
    part_z[sp] = part

    for k in range(chunks):
        core_write(k)

    remote(
        gram_in.at[pl.ds(0, 7)], rows_in.at[pl.ds(0, 7)], gz_send, gz_recv, sibling
    ).wait_recv()
    rows = rows_in[0]
    for j in range(1, 8):
        rows = rows + rows_in[j]
    tiles[me] = rows * scale_time
    swap = remote(tiles.at[me], tiles.at[me], gy_send, gy_recv, sibling)
    swap.start()

    remote(
        part_z.at[pl.ds(0, 7)], part_z.at[pl.ds(0, 7)], pz_send, pz_recv, sibling
    ).wait_recv()
    part = part_z[0]
    for j in range(1, 8):
        part = part + part_z[j]
    part = part * scale_param
    param_out[0:16, :] = part[:, :64]
    param_out[16:32, :] = part[:, 64:]

    swap.wait_recv()
    time_out[0:16, :] = tiles[0]
    time_out[16:32, :] = tiles[1]

    remote(
        sent.at[:, :, pl.ds(0, 3)], mid.at[:, :, pl.ds(0, 3)], x1_send, x1_recv.at[0, 0], sibling
    ).wait_send()
    remote(
        mid.at[:, :, pl.ds(0, 3)], held.at[:, :, pl.ds(0, 3)], x2_send, x2_recv.at[0], sibling
    ).wait_send()
    remote(
        core_sent.at[:, pl.ds(0, 15)], core_held.at[:, pl.ds(0, 15)],
        c_send, c_recv.at[0], sibling,
    ).wait_send()
    for k in range(chunks):
        remote(
            core_held.at[k], core_sib.at[k], cs_send.at[k], cs_recv.at[k], sibling
        ).wait_send()
    for dy in range(4):
        blocks = pl.ds(lax.rem(y + dy, 4) * 4, 4)
        remote(
            gram.at[blocks, 1 - me], gram_sib.at[blocks],
            gs_send.at[dy], gs_recv.at[dy], sibling,
        ).wait_send()
    remote(
        gram_sum.at[pl.ds(0, 15)], gram_in.at[pl.ds(0, 15)], g1_send, g1_recv, sibling
    ).wait_send()
    remote(
        gram_in.at[pl.ds(0, 7)], rows_in.at[pl.ds(0, 7)], gz_send, gz_recv, sibling
    ).wait_send()
    swap.wait_send()
    remote(
        part_in.at[pl.ds(0, 15)], part_in.at[pl.ds(0, 15)], px_send, px_recv, sibling
    ).wait_send()
    remote(
        part_z.at[pl.ds(0, 7)], part_z.at[pl.ds(0, 7)], pz_send, pz_recv, sibling
    ).wait_send()


def body(snapshots, time_basis):
    f32, bf16 = jnp.float32, jnp.bfloat16
    time_local, load_local, point_local = snapshots.shape
    columns = load_local * 2 * point_local * 8
    rank = time_basis.shape[1]
    k = point_local // LANE
    vmem = pltpu.VMEM
    dma = pltpu.SemaphoreType.DMA
    block = (k, 2, 4, 4, time_local, LANE)
    return pl.pallas_call(
        functools.partial(kernel, 1.0 / columns, 1.0 / (rank * point_local * 8)),
        out_shape=(
            jax.ShapeDtypeStruct((32, 512), f32),
            jax.ShapeDtypeStruct((4, 32, point_local), f32),
            jax.ShapeDtypeStruct((32, 64), f32),
        ),
        in_specs=[pl.BlockSpec(memory_space=pl.ANY), pl.BlockSpec(memory_space=vmem)],
        out_specs=(pl.BlockSpec(memory_space=vmem),) * 3,
        scratch_shapes=[
            vmem((k, time_local, load_local, LANE), f32),
            vmem(block, f32),
            vmem(block, f32),
            vmem(block, f32),
            vmem((512, 2 * LANE), bf16),
            vmem((512, 2 * LANE), bf16),
            vmem((2, 128, 512), bf16),
            vmem((2, 128, 512), bf16),
            vmem((16, 2, 16, 512), f32),
            vmem((16, 16, 512), f32),
            vmem((16, 16, 512), f32),
            vmem((16, 16, 512), f32),
            vmem((16, 512), f32),
            vmem((8, 16, 512), f32),
            vmem((2, 16, 512), f32),
            vmem((k, 16, 8, LANE), f32),
            vmem((k, 16, 8, LANE), f32),
            vmem((k, 16, 8, LANE), f32),
            vmem((2, 128, 128), f32),
            vmem((128, 128), f32),
            vmem((16, LANE), f32),
            vmem((16, 16, LANE), f32),
            vmem((16, LANE), f32),
            vmem((8, 16, LANE), f32),
            dma((k,)), dma, dma((k, 2)), dma, dma((k,)), dma, dma((k,)), dma((k,)), dma((k,)),
            dma((4,)), dma((4,)), dma, dma, dma, dma, dma, dma,
            dma, dma, dma, dma,
        ],
        compiler_params=pltpu.CompilerParams(
            collective_id=0, has_side_effects=True, vmem_limit_bytes=48 * 1024 * 1024
        ),
    )(snapshots, time_basis.T)


def solution(mesh):
    return jax.shard_map(
        body,
        mesh=mesh,
        in_specs=(P("tm", "param", "space"), P()),
        out_specs=(P("tm", None), P("tm", "param", "space"), P("param", None)),
        check_vma=False,
    )
```

```python
import functools

import jax
import jax.numpy as jnp
from jax import lax
from jax.experimental import pallas as pl
from jax.experimental.pallas import tpu as pltpu
from jax.sharding import PartitionSpec as P

MESH = pl.DeviceIdType.MESH
NT = (((1,), (1,)), ((), ()))
NN = (((1,), (0,)), ((), ()))
LANE = 128
ORDER = (
    (1, 0), (0, 1), (3, 0), (0, 3), (1, 1), (3, 3), (1, 3), (3, 1),
    (2, 0), (0, 2), (2, 1), (1, 2), (2, 3), (3, 2), (2, 2),
)


def dot(a, b, dims):
    return lax.dot_general(a, b, dims, preferred_element_type=jnp.float32)


def split(v):
    high = v.astype(jnp.bfloat16)
    return high, (v - high.astype(jnp.float32)).astype(jnp.bfloat16)


def split_3(v):
    high = v.astype(jnp.bfloat16)
    rest = v - high.astype(jnp.float32)
    return (high,) + split(rest)


def kernel(
    scale_time, scale_param,
    x_hbm, basis_hbm, time_out, core_out, param_out,
    basis_ref, staged, sent, mid, held, high_buf, low_buf, basis_high, basis_low,
    gram, gram_sib, gram_sum, gram_in, rows_mine, rows_in, tiles,
    core_sent, core_held, core_sib, pair_gram, pair_kept,
    part_mine, part_in, part_sum, part_z,
    relay, basis_sem, load_sem, x1_send, x1_recv, x2_send, x2_recv, c_send, c_recv, cs_send, cs_recv,
    gs_send, gs_recv, g1_send, g1_recv, gz_send, gz_recv, gy_send, gy_recv,
    px_send, px_recv, pz_send, pz_recv,
):
    sp, tm, me = lax.axis_index("space"), lax.axis_index("tm"), lax.axis_index("param")
    y, x = tm // 4, lax.rem(tm, 4)
    chunks, steps = staged.shape[0], staged.shape[1]

    def peer(dx, dy):
        return lax.rem(y + dy, 4) * 4 + lax.rem(x + dx, 4)

    def along(dz):
        return lax.rem(sp + dz, 8)

    def remote(src, dst, ssem, rsem, target):
        return pltpu.make_async_remote_copy(
            src_ref=src, dst_ref=dst, send_sem=ssem, recv_sem=rsem,
            device_id=target, device_id_type=MESH,
        )

    sibling = (sp, tm, 1 - me)
    ring = (1, 3, 2)
    far = (4, 3, 5, 2, 6, 1, 7)

    def load(k):
        return pltpu.make_async_copy(
            x_hbm.at[:, :, pl.ds(k * LANE, LANE)], staged.at[k], load_sem.at[k]
        )

    barrier = pltpu.get_barrier_semaphore()
    for d in (2, 1, 3):
        pl.semaphore_signal(barrier, inc=1, device_id=(sp, peer(d, 0), me), device_id_type=MESH)
        pl.semaphore_signal(barrier, inc=1, device_id=(sp, peer(0, d), me), device_id_type=MESH)
    for dz in (1, 7):
        pl.semaphore_signal(barrier, inc=1, device_id=(along(dz), tm, me), device_id_type=MESH)
    pl.semaphore_signal(barrier, inc=1, device_id=sibling, device_id_type=MESH)

    for k in range(chunks):
        load(k).start()
    basis_load = pltpu.make_async_copy(basis_hbm, basis_ref, basis_sem)
    basis_load.start()

    for k in range(chunks):
        load(k).wait()
        flat = staged.at[k].reshape(steps * steps, LANE)
        for j in range(16):
            for pp in range(2):
                sent[k, pp, j // 4, j % 4] = flat[pl.ds(2 * j + pp, steps, stride=steps), :]
        if k == 0:
            pl.semaphore_wait(barrier, 9)
        for d in ring:
            tx, ty = lax.rem(x + d, 4), lax.rem(y + d, 4)
            remote(
                sent.at[k, 0, :, tx], mid.at[k, 0, x], x1_send, x1_recv.at[k, 0],
                (sp, y * 4 + tx, me),
            ).start()
            remote(
                sent.at[k, 1, ty], mid.at[k, 1, y], x1_send, x1_recv.at[k, 1],
                (sp, ty * 4 + x, me),
            ).start()
        mid[k, 0, x] = sent[k, 0, :, x]
        mid[k, 1, y] = sent[k, 1, y]

    def pass_on(n):
        for dz in (1, 7):
            pl.semaphore_signal(
                relay.at[n], inc=1, device_id=(along(dz), tm, me), device_id_type=MESH
            )

    row = lax.broadcasted_iota(jnp.int32, (128, 64), 0)
    col = lax.broadcasted_iota(jnp.int32, (128, 64), 1)
    basis_load.wait()
    parts = split(basis_ref[...])
    for pp in range(2):
        pick = jnp.where(
            (lax.rem(row, 8) // 4 == pp) & (col == (row // 8) * 4 + lax.rem(row, 4)), 1.0, 0.0
        ).astype(jnp.bfloat16)
        basis_high[pp] = dot(pick, parts[0], NN).astype(jnp.bfloat16)
        basis_low[pp] = dot(pick, parts[1], NN).astype(jnp.bfloat16)

    gram[...] = jnp.zeros_like(gram)
    pair_gram[...] = jnp.zeros_like(pair_gram)

    for k in range(chunks):
        for pp in range(2):
            remote(
                sent.at[k, pp, pl.ds(0, 3)], mid.at[k, pp, pl.ds(0, 3)],
                x1_send, x1_recv.at[k, pp], sibling,
            ).wait_recv()
        for d in ring:
            tx, ty = lax.rem(x + d, 4), lax.rem(y + d, 4)
            remote(
                mid.at[k, 0, :, ty], held.at[k, 0, y], x2_send, x2_recv.at[k],
                (sp, ty * 4 + x, me),
            ).start()
            remote(
                mid.at[k, 1, :, tx], held.at[k, 1, :, x], x2_send, x2_recv.at[k],
                (sp, y * 4 + tx, me),
            ).start()
        held[k, 0, y] = mid[k, 0, :, y]
        held[k, 1, :, x] = mid[k, 1, :, x]

    def core_back(k):
        remote(
            core_sent.at[k, pl.ds(0, 15)], core_held.at[k, pl.ds(0, 15)],
            c_send, c_recv.at[k], sibling,
        ).wait_recv()
        remote(
            core_held.at[k], core_sib.at[k], cs_send.at[k], cs_recv.at[k], sibling
        ).start()

    def core_write(k):
        flat = core_held.at[k].reshape(128, LANE)
        for r in range(4):
            core_out[r, :, k * LANE:(k + 1) * LANE] = flat[pl.ds(r, 32, stride=4), :]

    def core_pair(k):
        remote(
            core_held.at[k], core_sib.at[k], cs_send.at[k], cs_recv.at[k], sibling
        ).wait_recv()
        high, low = split(core_held[k].reshape(128, LANE))
        high_2, low_2 = split(core_sib[k].reshape(128, LANE))
        pair_gram[0] += (dot(high, low, NT) + dot(low, high, NT)) + dot(high, high, NT)
        pair_gram[1] += (dot(high, low_2, NT) + dot(low, high_2, NT)) + dot(high, high_2, NT)

    for k in range(chunks):
        remote(
            mid.at[k, :, pl.ds(0, 3)], held.at[k, :, pl.ds(0, 3)],
            x2_send, x2_recv.at[k], sibling,
        ).wait_recv()
        for pp in range(2):
            high, low = split(held[k, pp].reshape(512, LANE))
            high_buf[:, pp * LANE:(pp + 1) * LANE] = high
            low_buf[:, pp * LANE:(pp + 1) * LANE] = low
        total = None
        for pp in range(2):
            high = high_buf[:, pp * LANE:(pp + 1) * LANE]
            low = low_buf[:, pp * LANE:(pp + 1) * LANE]
            term = (
                dot(basis_high[pp], low, NN) + dot(basis_low[pp], high, NN)
            ) + dot(basis_high[pp], high, NN)
            total = term if total is None else total + term
        core_sent[k] = total.reshape(16, 8, LANE)
        if 1 <= k <= 3:
            pl.semaphore_wait(relay.at[k - 1], 2)
        if k <= 2:
            pass_on(k)
        core_held[k, tm] = core_sent[k, tm]
        for dx, dy in ORDER:
            to = peer(dx, dy)
            remote(
                core_sent.at[k, to], core_held.at[k, tm], c_send, c_recv.at[k], (sp, to, me)
            ).start()
        for dy in range(4):
            there = lax.rem(y + dy, 4)
            rows = pl.ds(pl.multiple_of(there * 128, 128), 128)
            high, low = high_buf[rows, :], low_buf[rows, :]
            add = (
                dot(high, low_buf[...], NT) + dot(low, high_buf[...], NT)
            ) + dot(high, high_buf[...], NT)
            blocks = pl.ds(there * 4, 4)
            gram[blocks] = gram[blocks] + add.reshape(4, 2, 16, 512)
            if k == chunks - 1:
                remote(
                    gram.at[blocks, 1 - me], gram_sib.at[blocks],
                    gs_send.at[dy], gs_recv.at[dy], sibling,
                ).start()

    for dy in range(4):
        there = lax.rem(y + dy, 4)
        blocks = pl.ds(there * 4, 4)
        remote(
            gram.at[blocks, 1 - me], gram_sib.at[blocks],
            gs_send.at[dy], gs_recv.at[dy], sibling,
        ).wait_recv()
        gram_sum[blocks] = gram[blocks, me] + gram_sib[blocks]
        for dx in (1, 3, 2, 0):
            to = peer(dx, dy)
            if dx or dy:
                remote(
                    gram_sum.at[to], gram_in.at[tm], g1_send, g1_recv, (sp, to, me)
                ).start()
    gram_in[tm] = gram_sum[tm]

    for k in range(chunks):
        core_back(k)
    for k in range(chunks):
        core_pair(k)
    row = lax.broadcasted_iota(jnp.int32, (128, 128), 0)
    col = lax.broadcasted_iota(jnp.int32, (128, 128), 1)
    same = lax.rem(row, 4) == lax.rem(col, 4)
    row = lax.broadcasted_iota(jnp.int32, (64, 128), 0)
    col = lax.broadcasted_iota(jnp.int32, (64, 128), 1)
    part = jnp.zeros((32, 64), jnp.float32)
    for other in range(2):
        at = (1 - me) if other else me
        place = jnp.where(row == at * 32 + col // 4, 1.0, 0.0).astype(jnp.bfloat16)
        pair_kept[...] = jnp.where(same, pair_gram[other], 0.0)
        summed = (
            (pair_kept[pl.ds(0, 32, stride=4), :] + pair_kept[pl.ds(1, 32, stride=4), :])
            + (pair_kept[pl.ds(2, 32, stride=4), :] + pair_kept[pl.ds(3, 32, stride=4), :])
        )
        for small in split_3(summed):
            part = part + dot(small, place, NT)
    part_mine[...] = jnp.concatenate([part[:16], part[16:]], axis=1)
    for dx, dy in ORDER[::-1]:
        remote(
            part_mine, part_in.at[tm], px_send, px_recv, (sp, peer(dx, dy), me)
        ).start()
    part_in[tm] = part_mine[...]

    remote(
        gram_sum.at[pl.ds(0, 15)], gram_in.at[pl.ds(0, 15)], g1_send, g1_recv, sibling
    ).wait_recv()
    rows = gram_in[0]
    for j in range(1, 16):
        rows = rows + gram_in[j]
    rows_mine[...] = rows
    for dz in far:
        remote(
            rows_mine, rows_in.at[sp], gz_send, gz_recv, (along(dz), tm, me)
        ).start()
    rows_in[sp] = rows

    remote(
        part_in.at[pl.ds(0, 15)], part_in.at[pl.ds(0, 15)], px_send, px_recv, sibling
    ).wait_recv()
    part = part_in[0]
    for j in range(1, 16):
        part = part + part_in[j]
    part_sum[...] = part
    for dz in far:
        to = along(dz)
        remote(part_sum, part_z.at[sp], pz_send, pz_recv, (to, tm, me)).start()
    part_z[sp] = part

    for k in range(chunks):
        core_write(k)

    remote(
        gram_in.at[pl.ds(0, 7)], rows_in.at[pl.ds(0, 7)], gz_send, gz_recv, sibling
    ).wait_recv()
    rows = rows_in[0]
    for j in range(1, 8):
        rows = rows + rows_in[j]
    tiles[me] = rows * scale_time
    swap = remote(tiles.at[me], tiles.at[me], gy_send, gy_recv, sibling)
    swap.start()

    remote(
        part_z.at[pl.ds(0, 7)], part_z.at[pl.ds(0, 7)], pz_send, pz_recv, sibling
    ).wait_recv()
    part = part_z[0]
    for j in range(1, 8):
        part = part + part_z[j]
    part = part * scale_param
    param_out[0:16, :] = part[:, :64]
    param_out[16:32, :] = part[:, 64:]

    swap.wait_recv()
    time_out[0:16, :] = tiles[0]
    time_out[16:32, :] = tiles[1]

    remote(
        sent.at[:, :, pl.ds(0, 3)], mid.at[:, :, pl.ds(0, 3)], x1_send, x1_recv.at[0, 0], sibling
    ).wait_send()
    remote(
        mid.at[:, :, pl.ds(0, 3)], held.at[:, :, pl.ds(0, 3)], x2_send, x2_recv.at[0], sibling
    ).wait_send()
    remote(
        core_sent.at[:, pl.ds(0, 15)], core_held.at[:, pl.ds(0, 15)],
        c_send, c_recv.at[0], sibling,
    ).wait_send()
    for k in range(chunks):
        remote(
            core_held.at[k], core_sib.at[k], cs_send.at[k], cs_recv.at[k], sibling
        ).wait_send()
    for dy in range(4):
        blocks = pl.ds(lax.rem(y + dy, 4) * 4, 4)
        remote(
            gram.at[blocks, 1 - me], gram_sib.at[blocks],
            gs_send.at[dy], gs_recv.at[dy], sibling,
        ).wait_send()
    remote(
        gram_sum.at[pl.ds(0, 15)], gram_in.at[pl.ds(0, 15)], g1_send, g1_recv, sibling
    ).wait_send()
    remote(
        gram_in.at[pl.ds(0, 7)], rows_in.at[pl.ds(0, 7)], gz_send, gz_recv, sibling
    ).wait_send()
    swap.wait_send()
    remote(
        part_in.at[pl.ds(0, 15)], part_in.at[pl.ds(0, 15)], px_send, px_recv, sibling
    ).wait_send()
    remote(
        part_z.at[pl.ds(0, 7)], part_z.at[pl.ds(0, 7)], pz_send, pz_recv, sibling
    ).wait_send()


def body(snapshots, time_basis):
    f32, bf16 = jnp.float32, jnp.bfloat16
    time_local, load_local, point_local = snapshots.shape
    columns = load_local * 2 * point_local * 8
    rank = time_basis.shape[1]
    k = point_local // LANE
    vmem = pltpu.VMEM
    dma = pltpu.SemaphoreType.DMA
    block = (k, 2, 4, 4, time_local, LANE)
    return pl.pallas_call(
        functools.partial(kernel, 1.0 / columns, 1.0 / (rank * point_local * 8)),
        out_shape=(
            jax.ShapeDtypeStruct((32, 512), f32),
            jax.ShapeDtypeStruct((4, 32, point_local), f32),
            jax.ShapeDtypeStruct((32, 64), f32),
        ),
        in_specs=[pl.BlockSpec(memory_space=pl.ANY)] * 2,
        out_specs=(pl.BlockSpec(memory_space=vmem),) * 3,
        scratch_shapes=[
            vmem((rank, 512), f32),
            vmem((k, time_local, load_local, LANE), f32),
            vmem(block, f32),
            vmem(block, f32),
            vmem(block, f32),
            vmem((512, 2 * LANE), bf16),
            vmem((512, 2 * LANE), bf16),
            vmem((2, 128, 512), bf16),
            vmem((2, 128, 512), bf16),
            vmem((16, 2, 16, 512), f32),
            vmem((16, 16, 512), f32),
            vmem((16, 16, 512), f32),
            vmem((16, 16, 512), f32),
            vmem((16, 512), f32),
            vmem((8, 16, 512), f32),
            vmem((2, 16, 512), f32),
            vmem((k, 16, 8, LANE), f32),
            vmem((k, 16, 8, LANE), f32),
            vmem((k, 16, 8, LANE), f32),
            vmem((2, 128, 128), f32),
            vmem((128, 128), f32),
            vmem((16, LANE), f32),
            vmem((16, 16, LANE), f32),
            vmem((16, LANE), f32),
            vmem((8, 16, LANE), f32),
            pltpu.SemaphoreType.REGULAR((3,)),
            dma, dma((k,)), dma, dma((k, 2)), dma, dma((k,)), dma, dma((k,)), dma((k,)), dma((k,)),
            dma((4,)), dma((4,)), dma, dma, dma, dma, dma, dma,
            dma, dma, dma, dma,
        ],
        compiler_params=pltpu.CompilerParams(
            collective_id=0, has_side_effects=True, vmem_limit_bytes=40 * 1024 * 1024
        ),
    )(
        pltpu.with_memory_space_constraint(snapshots, pltpu.HBM),
        pltpu.with_memory_space_constraint(time_basis.T, pltpu.HBM),
    )


def solution(mesh):
    return jax.shard_map(
        body,
        mesh=mesh,
        in_specs=(P("tm", "param", "space"), P()),
        out_specs=(P("tm", None), P("tm", "param", "space"), P("param", None)),
        check_vma=False,
    )
```

```python
import functools

import jax
import jax.numpy as jnp
from jax import lax
from jax.experimental import pallas as pl
from jax.experimental.pallas import tpu as pltpu
from jax.sharding import PartitionSpec as P

MESH = pl.DeviceIdType.MESH
NT = (((1,), (1,)), ((), ()))
NN = (((1,), (0,)), ((), ()))
LANE = 128
ORDER = (
    (1, 0), (0, 1), (3, 0), (0, 3), (1, 1), (3, 3), (1, 3), (3, 1),
    (2, 0), (0, 2), (2, 1), (1, 2), (2, 3), (3, 2), (2, 2),
)


def dot(a, b, dims):
    return lax.dot_general(a, b, dims, preferred_element_type=jnp.float32)


def split(v):
    high = v.astype(jnp.bfloat16)
    return high, (v - high.astype(jnp.float32)).astype(jnp.bfloat16)


def split_3(v):
    high = v.astype(jnp.bfloat16)
    rest = v - high.astype(jnp.float32)
    return (high,) + split(rest)


def kernel(
    scale_time, scale_param,
    x_hbm, basis_hbm, time_out, core_out, param_out,
    basis_ref, staged, sent, mid, held, held_sib, high_buf, low_buf, basis_high, basis_low,
    gram, gram_in, rows_mine, rows_in, tiles,
    core_sent, core_held, core_sib, pair_gram, pair_kept,
    part_mine, part_in, part_sum, part_z,
    relay, basis_sem, load_sem, x1_send, x1_recv, x2_send, x2_recv, c_send, c_recv, cs_send, cs_recv,
    f_send, f_recv, g1_send, g1_recv, gz_send, gz_recv, gy_send, gy_recv,
    px_send, px_recv, pz_send, pz_recv,
):
    sp, tm, me = lax.axis_index("space"), lax.axis_index("tm"), lax.axis_index("param")
    y, x = tm // 4, lax.rem(tm, 4)
    chunks, steps = staged.shape[0], staged.shape[1]

    def peer(dx, dy):
        return lax.rem(y + dy, 4) * 4 + lax.rem(x + dx, 4)

    def along(dz):
        return lax.rem(sp + dz, 8)

    def remote(src, dst, ssem, rsem, target):
        return pltpu.make_async_remote_copy(
            src_ref=src, dst_ref=dst, send_sem=ssem, recv_sem=rsem,
            device_id=target, device_id_type=MESH,
        )

    sibling = (sp, tm, 1 - me)
    ring = (1, 3, 2)
    far = (4, 3, 5, 2, 6, 1, 7)

    def load(k):
        return pltpu.make_async_copy(
            x_hbm.at[:, :, pl.ds(k * LANE, LANE)], staged.at[k], load_sem.at[k]
        )

    barrier = pltpu.get_barrier_semaphore()
    for d in (2, 1, 3):
        pl.semaphore_signal(barrier, inc=1, device_id=(sp, peer(d, 0), me), device_id_type=MESH)
        pl.semaphore_signal(barrier, inc=1, device_id=(sp, peer(0, d), me), device_id_type=MESH)
    for dz in (1, 7):
        pl.semaphore_signal(barrier, inc=1, device_id=(along(dz), tm, me), device_id_type=MESH)
    pl.semaphore_signal(barrier, inc=1, device_id=sibling, device_id_type=MESH)

    for k in range(chunks):
        load(k).start()
    basis_load = pltpu.make_async_copy(basis_hbm, basis_ref, basis_sem)
    basis_load.start()

    for k in range(chunks):
        load(k).wait()
        flat = staged.at[k].reshape(steps * steps, LANE)
        for j in range(16):
            for pp in range(2):
                sent[k, pp, j // 4, j % 4] = flat[pl.ds(2 * j + pp, steps, stride=steps), :]
        if k == 0:
            pl.semaphore_wait(barrier, 9)
        for d in ring:
            tx, ty = lax.rem(x + d, 4), lax.rem(y + d, 4)
            remote(
                sent.at[k, 0, :, tx], mid.at[k, 0, x], x1_send, x1_recv.at[k, 0],
                (sp, y * 4 + tx, me),
            ).start()
            remote(
                sent.at[k, 1, ty], mid.at[k, 1, y], x1_send, x1_recv.at[k, 1],
                (sp, ty * 4 + x, me),
            ).start()
        mid[k, 0, x] = sent[k, 0, :, x]
        mid[k, 1, y] = sent[k, 1, y]

    def pass_on(n):
        for dz in (1, 7):
            pl.semaphore_signal(
                relay.at[n], inc=1, device_id=(along(dz), tm, me), device_id_type=MESH
            )

    row = lax.broadcasted_iota(jnp.int32, (128, 64), 0)
    col = lax.broadcasted_iota(jnp.int32, (128, 64), 1)
    basis_load.wait()
    parts = split(basis_ref[...])
    for pp in range(2):
        pick = jnp.where(
            (lax.rem(row, 8) // 4 == pp) & (col == (row // 8) * 4 + lax.rem(row, 4)), 1.0, 0.0
        ).astype(jnp.bfloat16)
        basis_high[pp] = dot(pick, parts[0], NN).astype(jnp.bfloat16)
        basis_low[pp] = dot(pick, parts[1], NN).astype(jnp.bfloat16)

    gram[...] = jnp.zeros_like(gram)
    pair_gram[...] = jnp.zeros_like(pair_gram)

    for k in range(chunks):
        for pp in range(2):
            remote(
                sent.at[k, pp, pl.ds(0, 3)], mid.at[k, pp, pl.ds(0, 3)],
                x1_send, x1_recv.at[k, pp], sibling,
            ).wait_recv()
        for d in ring:
            tx, ty = lax.rem(x + d, 4), lax.rem(y + d, 4)
            remote(
                mid.at[k, 0, :, ty], held.at[k, 0, y], x2_send, x2_recv.at[k],
                (sp, ty * 4 + x, me),
            ).start()
            remote(
                mid.at[k, 1, :, tx], held.at[k, 1, :, x], x2_send, x2_recv.at[k],
                (sp, y * 4 + tx, me),
            ).start()
        held[k, 0, y] = mid[k, 0, :, y]
        held[k, 1, :, x] = mid[k, 1, :, x]

    def core_back(k):
        remote(
            core_sent.at[k, pl.ds(0, 15)], core_held.at[k, pl.ds(0, 15)],
            c_send, c_recv.at[k], sibling,
        ).wait_recv()
        remote(
            core_held.at[k], core_sib.at[k], cs_send.at[k], cs_recv.at[k], sibling
        ).start()

    def core_write(k):
        flat = core_held.at[k].reshape(128, LANE)
        for r in range(4):
            core_out[r, :, k * LANE:(k + 1) * LANE] = flat[pl.ds(r, 32, stride=4), :]

    def core_pair(k):
        remote(
            core_held.at[k], core_sib.at[k], cs_send.at[k], cs_recv.at[k], sibling
        ).wait_recv()
        high, low = split(core_held[k].reshape(128, LANE))
        high_2, low_2 = split(core_sib[k].reshape(128, LANE))
        pair_gram[0] += (dot(high, low, NT) + dot(low, high, NT)) + dot(high, high, NT)
        pair_gram[1] += (dot(high, low_2, NT) + dot(low, high_2, NT)) + dot(high, high_2, NT)

    def forward(k):
        return remote(held.at[k], held_sib.at[k], f_send.at[k], f_recv.at[k], sibling)

    def convert(blocks, k):
        for pp in range(2):
            high, low = split(blocks[k, pp].reshape(16, 2, 16, LANE))
            high_buf[:, :, :, pp * LANE:(pp + 1) * LANE] = high
            low_buf[:, :, :, pp * LANE:(pp + 1) * LANE] = low

    def add_gram():
        all_high = high_buf[...].reshape(512, 2 * LANE)
        all_low = low_buf[...].reshape(512, 2 * LANE)
        high = high_buf[:, me].reshape(256, 2 * LANE)
        low = low_buf[:, me].reshape(256, 2 * LANE)
        add = (dot(high, all_low, NT) + dot(low, all_high, NT)) + dot(high, all_high, NT)
        add = add.reshape(16, 2, 8, 512)
        gram[:, 0:2] += add[:, :, :, :256]
        gram[:, 2:4] += add[:, :, :, 256:]

    for k in range(chunks):
        remote(
            mid.at[k, :, pl.ds(0, 3)], held.at[k, :, pl.ds(0, 3)],
            x2_send, x2_recv.at[k], sibling,
        ).wait_recv()
        forward(k).start()
        convert(held, k)
        total = None
        for pp in range(2):
            high = high_buf[:, :, :, pp * LANE:(pp + 1) * LANE].reshape(512, LANE)
            low = low_buf[:, :, :, pp * LANE:(pp + 1) * LANE].reshape(512, LANE)
            term = (
                dot(basis_high[pp], low, NN) + dot(basis_low[pp], high, NN)
            ) + dot(basis_high[pp], high, NN)
            total = term if total is None else total + term
        core_sent[k] = total.reshape(16, 8, LANE)
        if 1 <= k <= 4:
            pl.semaphore_wait(relay.at[k - 1], 2)
        if k <= 3:
            pass_on(k)
        core_held[k, tm] = core_sent[k, tm]
        for dx, dy in ORDER:
            to = peer(dx, dy)
            remote(
                core_sent.at[k, to], core_held.at[k, tm], c_send, c_recv.at[k], (sp, to, me)
            ).start()
        add_gram()
        forward(k).wait_recv()
        convert(held_sib, k)
        add_gram()

    for h in range(4):
        for dx, dy in ORDER:
            to = peer(dx, dy)
            remote(
                gram.at[to, h], gram_in.at[h, tm], g1_send, g1_recv.at[h], (sp, to, me)
            ).start()
        gram_in[h, tm] = gram[tm, h]

    for k in range(chunks):
        core_back(k)
    for k in range(chunks):
        core_pair(k)
    row = lax.broadcasted_iota(jnp.int32, (128, 128), 0)
    col = lax.broadcasted_iota(jnp.int32, (128, 128), 1)
    same = lax.rem(row, 4) == lax.rem(col, 4)
    row = lax.broadcasted_iota(jnp.int32, (64, 128), 0)
    col = lax.broadcasted_iota(jnp.int32, (64, 128), 1)
    part = jnp.zeros((32, 64), jnp.float32)
    for other in range(2):
        at = (1 - me) if other else me
        place = jnp.where(row == at * 32 + col // 4, 1.0, 0.0).astype(jnp.bfloat16)
        pair_kept[...] = jnp.where(same, pair_gram[other], 0.0)
        summed = (
            (pair_kept[pl.ds(0, 32, stride=4), :] + pair_kept[pl.ds(1, 32, stride=4), :])
            + (pair_kept[pl.ds(2, 32, stride=4), :] + pair_kept[pl.ds(3, 32, stride=4), :])
        )
        for small in split_3(summed):
            part = part + dot(small, place, NT)
    part_mine[...] = jnp.concatenate([part[:16], part[16:]], axis=1)
    for dx, dy in ORDER[::-1]:
        remote(
            part_mine, part_in.at[tm], px_send, px_recv, (sp, peer(dx, dy), me)
        ).start()
    part_in[tm] = part_mine[...]

    for h in range(4):
        remote(
            gram.at[pl.ds(0, 15), h], gram_in.at[h, pl.ds(0, 15)],
            g1_send, g1_recv.at[h], sibling,
        ).wait_recv()
        rows = gram_in[h, 0]
        for j in range(1, 16):
            rows = rows + gram_in[h, j]
        rows_mine[h] = rows
        for dz in far + (0,):
            remote(
                rows_mine.at[h], rows_in.at[h, sp], gz_send, gz_recv.at[h],
                (along(dz), tm, 1 - me),
            ).start()

    remote(
        part_in.at[pl.ds(0, 15)], part_in.at[pl.ds(0, 15)], px_send, px_recv, sibling
    ).wait_recv()
    part = part_in[0]
    for j in range(1, 16):
        part = part + part_in[j]
    part_sum[...] = part
    for dz in far:
        to = along(dz)
        remote(part_sum, part_z.at[sp], pz_send, pz_recv, (to, tm, me)).start()
    part_z[sp] = part

    for k in range(chunks):
        core_write(k)

    for h in range(4):
        remote(
            gram_in.at[h, pl.ds(0, 8)], rows_in.at[h], gz_send, gz_recv.at[h], sibling
        ).wait_recv()
        rows = rows_in[h, 0]
        for j in range(1, 8):
            rows = rows + rows_in[h, j]
        tiles[1 - me, (h % 2) * 8:(h % 2) * 8 + 8, (h // 2) * 256:(h // 2) * 256 + 256] = rows * scale_time
    swap = remote(tiles.at[1 - me], tiles.at[1 - me], gy_send, gy_recv, sibling)
    swap.start()

    remote(
        part_z.at[pl.ds(0, 7)], part_z.at[pl.ds(0, 7)], pz_send, pz_recv, sibling
    ).wait_recv()
    part = part_z[0]
    for j in range(1, 8):
        part = part + part_z[j]
    part = part * scale_param
    param_out[0:16, :] = part[:, :64]
    param_out[16:32, :] = part[:, 64:]

    swap.wait_recv()
    time_out[0:16, :] = tiles[0]
    time_out[16:32, :] = tiles[1]

    remote(
        sent.at[:, :, pl.ds(0, 3)], mid.at[:, :, pl.ds(0, 3)], x1_send, x1_recv.at[0, 0], sibling
    ).wait_send()
    remote(
        mid.at[:, :, pl.ds(0, 3)], held.at[:, :, pl.ds(0, 3)], x2_send, x2_recv.at[0], sibling
    ).wait_send()
    remote(
        core_sent.at[:, pl.ds(0, 15)], core_held.at[:, pl.ds(0, 15)],
        c_send, c_recv.at[0], sibling,
    ).wait_send()
    for k in range(chunks):
        remote(
            core_held.at[k], core_sib.at[k], cs_send.at[k], cs_recv.at[k], sibling
        ).wait_send()
    for k in range(chunks):
        forward(k).wait_send()
    remote(
        gram.at[pl.ds(0, 15)], gram.at[pl.ds(0, 15)], g1_send, g1_recv.at[0], sibling
    ).wait_send()
    remote(rows_in, rows_in, gz_send, gz_recv.at[0], sibling).wait_send()
    swap.wait_send()
    remote(
        part_in.at[pl.ds(0, 15)], part_in.at[pl.ds(0, 15)], px_send, px_recv, sibling
    ).wait_send()
    remote(
        part_z.at[pl.ds(0, 7)], part_z.at[pl.ds(0, 7)], pz_send, pz_recv, sibling
    ).wait_send()


def body(snapshots, time_basis):
    f32, bf16 = jnp.float32, jnp.bfloat16
    time_local, load_local, point_local = snapshots.shape
    columns = load_local * 2 * point_local * 8
    rank = time_basis.shape[1]
    k = point_local // LANE
    vmem = pltpu.VMEM
    dma = pltpu.SemaphoreType.DMA
    block = (k, 2, 4, 4, time_local, LANE)
    return pl.pallas_call(
        functools.partial(kernel, 1.0 / columns, 1.0 / (rank * point_local * 8)),
        out_shape=(
            jax.ShapeDtypeStruct((32, 512), f32),
            jax.ShapeDtypeStruct((4, 32, point_local), f32),
            jax.ShapeDtypeStruct((32, 64), f32),
        ),
        in_specs=[pl.BlockSpec(memory_space=pl.ANY)] * 2,
        out_specs=(pl.BlockSpec(memory_space=vmem),) * 3,
        scratch_shapes=[
            vmem((rank, 512), f32),
            vmem((k, time_local, load_local, LANE), f32),
            vmem(block, f32),
            vmem(block, f32),
            vmem(block, f32),
            vmem(block, f32),
            vmem((16, 2, 16, 2 * LANE), bf16),
            vmem((16, 2, 16, 2 * LANE), bf16),
            vmem((2, 128, 512), bf16),
            vmem((2, 128, 512), bf16),
            vmem((16, 4, 8, 256), f32),
            vmem((4, 16, 8, 256), f32),
            vmem((4, 8, 256), f32),
            vmem((4, 8, 8, 256), f32),
            vmem((2, 16, 512), f32),
            vmem((k, 16, 8, LANE), f32),
            vmem((k, 16, 8, LANE), f32),
            vmem((k, 16, 8, LANE), f32),
            vmem((2, 128, 128), f32),
            vmem((128, 128), f32),
            vmem((16, LANE), f32),
            vmem((16, 16, LANE), f32),
            vmem((16, LANE), f32),
            vmem((8, 16, LANE), f32),
            pltpu.SemaphoreType.REGULAR((4,)),
            dma, dma((k,)), dma, dma((k, 2)), dma, dma((k,)), dma, dma((k,)), dma((k,)), dma((k,)),
            dma((k,)), dma((k,)), dma, dma((4,)), dma, dma((4,)), dma, dma,
            dma, dma, dma, dma,
        ],
        compiler_params=pltpu.CompilerParams(
            collective_id=0, has_side_effects=True, vmem_limit_bytes=40 * 1024 * 1024
        ),
    )(
        pltpu.with_memory_space_constraint(snapshots, pltpu.HBM),
        pltpu.with_memory_space_constraint(time_basis.T, pltpu.HBM),
    )


def solution(mesh):
    return jax.shard_map(
        body,
        mesh=mesh,
        in_specs=(P("tm", "param", "space"), P()),
        out_specs=(P("tm", None), P("tm", "param", "space"), P("param", None)),
        check_vma=False,
    )
```

```python
import functools

import jax
import jax.numpy as jnp
from jax import lax
from jax.experimental import pallas as pl
from jax.experimental.pallas import tpu as pltpu
from jax.sharding import PartitionSpec as P

MESH = pl.DeviceIdType.MESH
NT = (((1,), (1,)), ((), ()))
NN = (((1,), (0,)), ((), ()))
LANE = 128
ORDER = (
    (1, 0), (0, 1), (3, 0), (0, 3), (1, 1), (3, 3), (1, 3), (3, 1),
    (2, 0), (0, 2), (2, 1), (1, 2), (2, 3), (3, 2), (2, 2),
)


def dot(a, b, dims):
    return lax.dot_general(a, b, dims, preferred_element_type=jnp.float32)


def split(v):
    high = v.astype(jnp.bfloat16)
    return high, (v - high.astype(jnp.float32)).astype(jnp.bfloat16)


def split_3(v):
    high = v.astype(jnp.bfloat16)
    rest = v - high.astype(jnp.float32)
    return (high,) + split(rest)


def kernel(
    scale_time, scale_param,
    x_hbm, basis_hbm, time_out, core_out, param_out,
    basis_ref, staged, sent, mid, held, held_sib, high_buf, low_buf, basis_high, basis_low,
    gram, gram_in, rows_mine, rows_in, tiles,
    core_sent, core_held, core_sib, pair_gram, pair_kept,
    part_mine, part_in, part_sum, part_z,
    relay, basis_sem, load_sem, x1_send, x1_recv, x2_send, x2_recv, c_send, c_recv, cs_send, cs_recv,
    f_send, f_recv, g1_send, g1_recv, gz_send, gz_recv, gy_send, gy_recv,
    px_send, px_recv, pz_send, pz_recv,
):
    sp, tm, me = lax.axis_index("space"), lax.axis_index("tm"), lax.axis_index("param")
    y, x = tm // 4, lax.rem(tm, 4)
    chunks, steps = staged.shape[0], staged.shape[1]

    def peer(dx, dy):
        return lax.rem(y + dy, 4) * 4 + lax.rem(x + dx, 4)

    def along(dz):
        return lax.rem(sp + dz, 8)

    def remote(src, dst, ssem, rsem, target):
        return pltpu.make_async_remote_copy(
            src_ref=src, dst_ref=dst, send_sem=ssem, recv_sem=rsem,
            device_id=target, device_id_type=MESH,
        )

    sibling = (sp, tm, 1 - me)
    ring = (1, 3, 2)
    far = (4, 3, 5, 2, 6, 1, 7)

    def load(k):
        return pltpu.make_async_copy(
            x_hbm.at[:, :, pl.ds(k * LANE, LANE)], staged.at[k], load_sem.at[k]
        )

    barrier = pltpu.get_barrier_semaphore()
    for d in (2, 1, 3):
        pl.semaphore_signal(barrier, inc=1, device_id=(sp, peer(d, 0), me), device_id_type=MESH)
        pl.semaphore_signal(barrier, inc=1, device_id=(sp, peer(0, d), me), device_id_type=MESH)
    for dz in (1, 7):
        pl.semaphore_signal(barrier, inc=1, device_id=(along(dz), tm, me), device_id_type=MESH)
    pl.semaphore_signal(barrier, inc=1, device_id=sibling, device_id_type=MESH)

    for k in range(chunks):
        load(k).start()
    basis_load = pltpu.make_async_copy(basis_hbm, basis_ref, basis_sem)
    basis_load.start()

    for k in range(chunks):
        load(k).wait()
        flat = staged.at[k].reshape(steps * steps, LANE)
        for j in range(16):
            for pp in range(2):
                sent[k, pp, j // 4, j % 4] = flat[pl.ds(2 * j + pp, steps, stride=steps), :]
        if k == 0:
            pl.semaphore_wait(barrier, 9)
        for d in ring:
            tx, ty = lax.rem(x + d, 4), lax.rem(y + d, 4)
            remote(
                sent.at[k, 0, :, tx], mid.at[k, 0, x], x1_send, x1_recv.at[k, 0],
                (sp, y * 4 + tx, me),
            ).start()
            remote(
                sent.at[k, 1, ty], mid.at[k, 1, y], x1_send, x1_recv.at[k, 1],
                (sp, ty * 4 + x, me),
            ).start()
        mid[k, 0, x] = sent[k, 0, :, x]
        mid[k, 1, y] = sent[k, 1, y]

    def pass_on(n):
        for dz in (1, 7):
            pl.semaphore_signal(
                relay.at[n], inc=1, device_id=(along(dz), tm, me), device_id_type=MESH
            )

    row = lax.broadcasted_iota(jnp.int32, (128, 64), 0)
    col = lax.broadcasted_iota(jnp.int32, (128, 64), 1)
    basis_load.wait()
    parts = split(basis_ref[...])
    for pp in range(2):
        pick = jnp.where(
            (lax.rem(row, 8) // 4 == pp) & (col == (row // 8) * 4 + lax.rem(row, 4)), 1.0, 0.0
        ).astype(jnp.bfloat16)
        basis_high[pp] = dot(pick, parts[0], NN).astype(jnp.bfloat16)
        basis_low[pp] = dot(pick, parts[1], NN).astype(jnp.bfloat16)

    gram[...] = jnp.zeros_like(gram)
    pair_gram[...] = jnp.zeros_like(pair_gram)

    for k in range(chunks):
        for pp in range(2):
            remote(
                sent.at[k, pp, pl.ds(0, 3)], mid.at[k, pp, pl.ds(0, 3)],
                x1_send, x1_recv.at[k, pp], sibling,
            ).wait_recv()
        for d in ring:
            tx, ty = lax.rem(x + d, 4), lax.rem(y + d, 4)
            remote(
                mid.at[k, 0, :, ty], held.at[k, 0, y], x2_send, x2_recv.at[k],
                (sp, ty * 4 + x, me),
            ).start()
            remote(
                mid.at[k, 1, :, tx], held.at[k, 1, :, x], x2_send, x2_recv.at[k],
                (sp, y * 4 + tx, me),
            ).start()
        held[k, 0, y] = mid[k, 0, :, y]
        held[k, 1, :, x] = mid[k, 1, :, x]

    def core_back(k):
        remote(
            core_sent.at[k, pl.ds(0, 15)], core_held.at[k, pl.ds(0, 15)],
            c_send, c_recv.at[k], sibling,
        ).wait_recv()
        remote(
            core_held.at[k], core_sib.at[k], cs_send.at[k], cs_recv.at[k], sibling
        ).start()

    def core_write(k):
        flat = core_held.at[k].reshape(128, LANE)
        for r in range(4):
            core_out[r, :, k * LANE:(k + 1) * LANE] = flat[pl.ds(r, 32, stride=4), :]

    def core_pair(k):
        remote(
            core_held.at[k], core_sib.at[k], cs_send.at[k], cs_recv.at[k], sibling
        ).wait_recv()
        high, low = split(core_held[k].reshape(128, LANE))
        high_2, low_2 = split(core_sib[k].reshape(128, LANE))
        pair_gram[0] += (dot(high, low, NT) + dot(low, high, NT)) + dot(high, high, NT)
        pair_gram[1] += (dot(high, low_2, NT) + dot(low, high_2, NT)) + dot(high, high_2, NT)

    def forward(k):
        return remote(held.at[k], held_sib.at[k], f_send.at[k], f_recv.at[k], sibling)

    def convert(blocks, k):
        for pp in range(2):
            high, low = split(blocks[k, pp].reshape(16, 2, 16, LANE))
            high_buf[:, :, :, pp * LANE:(pp + 1) * LANE] = high
            low_buf[:, :, :, pp * LANE:(pp + 1) * LANE] = low

    def add_gram():
        all_high = high_buf[...].reshape(512, 2 * LANE)
        all_low = low_buf[...].reshape(512, 2 * LANE)
        high = high_buf[:, me].reshape(256, 2 * LANE)
        low = low_buf[:, me].reshape(256, 2 * LANE)
        add = (dot(high, all_low, NT) + dot(low, all_high, NT)) + dot(high, all_high, NT)
        add = add.reshape(16, 2, 8, 512)
        gram[:, 0:2] += add[:, :, :, :256]
        gram[:, 2:4] += add[:, :, :, 256:]

    for k in range(chunks):
        remote(
            mid.at[k, :, pl.ds(0, 3)], held.at[k, :, pl.ds(0, 3)],
            x2_send, x2_recv.at[k], sibling,
        ).wait_recv()
        forward(k).start()
        convert(held, k)
        total = None
        for pp in range(2):
            high = high_buf[:, :, :, pp * LANE:(pp + 1) * LANE].reshape(512, LANE)
            low = low_buf[:, :, :, pp * LANE:(pp + 1) * LANE].reshape(512, LANE)
            term = (
                dot(basis_high[pp], low, NN) + dot(basis_low[pp], high, NN)
            ) + dot(basis_high[pp], high, NN)
            total = term if total is None else total + term
        core_sent[k] = total.reshape(16, 8, LANE)
        if 1 <= k <= 4:
            pl.semaphore_wait(relay.at[k - 1], 2)
        if k <= 3:
            pass_on(k)
        core_held[k, tm] = core_sent[k, tm]
        for dx, dy in ORDER:
            to = peer(dx, dy)
            remote(
                core_sent.at[k, to], core_held.at[k, tm], c_send, c_recv.at[k], (sp, to, me)
            ).start()
        add_gram()
        forward(k).wait_recv()
        convert(held_sib, k)
        add_gram()

    for h in range(4):
        for dx, dy in ORDER:
            to = peer(dx, dy)
            remote(
                gram.at[to, h], gram_in.at[h, tm], g1_send, g1_recv.at[h], (sp, to, me)
            ).start()
        gram_in[h, tm] = gram[tm, h]

    for k in range(chunks):
        core_back(k)
    for k in range(chunks):
        core_pair(k)
    row = lax.broadcasted_iota(jnp.int32, (128, 128), 0)
    col = lax.broadcasted_iota(jnp.int32, (128, 128), 1)
    same = lax.rem(row, 4) == lax.rem(col, 4)
    row = lax.broadcasted_iota(jnp.int32, (64, 128), 0)
    col = lax.broadcasted_iota(jnp.int32, (64, 128), 1)
    part = jnp.zeros((32, 64), jnp.float32)
    for other in range(2):
        at = (1 - me) if other else me
        place = jnp.where(row == at * 32 + col // 4, 1.0, 0.0).astype(jnp.bfloat16)
        pair_kept[...] = jnp.where(same, pair_gram[other], 0.0)
        summed = (
            (pair_kept[pl.ds(0, 32, stride=4), :] + pair_kept[pl.ds(1, 32, stride=4), :])
            + (pair_kept[pl.ds(2, 32, stride=4), :] + pair_kept[pl.ds(3, 32, stride=4), :])
        )
        for small in split_3(summed):
            part = part + dot(small, place, NT)
    part_mine[...] = jnp.concatenate([part[:16], part[16:]], axis=1)
    for dx, dy in ORDER[::-1]:
        remote(
            part_mine, part_in.at[tm], px_send, px_recv, (sp, peer(dx, dy), me)
        ).start()
    part_in[tm] = part_mine[...]

    for h in range(4):
        remote(
            gram.at[pl.ds(0, 15), h], gram_in.at[h, pl.ds(0, 15)],
            g1_send, g1_recv.at[h], sibling,
        ).wait_recv()
        rows = gram_in[h, 0]
        for j in range(1, 16):
            rows = rows + gram_in[h, j]
        rows_mine[h] = rows
        for dz in far + (0,):
            remote(
                rows_mine.at[h], rows_in.at[h, sp], gz_send, gz_recv.at[h],
                (along(dz), tm, 1 - me),
            ).start()

    remote(
        part_in.at[pl.ds(0, 15)], part_in.at[pl.ds(0, 15)], px_send, px_recv, sibling
    ).wait_recv()
    part = part_in[0]
    for j in range(1, 16):
        part = part + part_in[j]
    part_sum[...] = part
    for dz in far:
        to = along(dz)
        remote(part_sum, part_z.at[sp], pz_send, pz_recv, (to, tm, me)).start()
    part_z[sp] = part

    for k in range(chunks):
        core_write(k)

    for h in range(4):
        remote(
            gram_in.at[h, pl.ds(0, 8)], rows_in.at[h], gz_send, gz_recv.at[h], sibling
        ).wait_recv()
        rows = rows_in[h, 0]
        for j in range(1, 8):
            rows = rows + rows_in[h, j]
        tiles[1 - me, (h % 2) * 8:(h % 2) * 8 + 8, (h // 2) * 256:(h // 2) * 256 + 256] = rows * scale_time
    swap = remote(tiles.at[1 - me], tiles.at[1 - me], gy_send, gy_recv, sibling)
    swap.start()

    remote(
        part_z.at[pl.ds(0, 7)], part_z.at[pl.ds(0, 7)], pz_send, pz_recv, sibling
    ).wait_recv()
    part = part_z[0]
    for j in range(1, 8):
        part = part + part_z[j]
    part = part * scale_param
    param_out[0:16, :] = part[:, :64]
    param_out[16:32, :] = part[:, 64:]

    swap.wait_recv()
    time_out[0:16, :] = tiles[0]
    time_out[16:32, :] = tiles[1]

    remote(
        sent.at[:, :, pl.ds(0, 3)], mid.at[:, :, pl.ds(0, 3)], x1_send, x1_recv.at[0, 0], sibling
    ).wait_send()
    remote(
        mid.at[:, :, pl.ds(0, 3)], held.at[:, :, pl.ds(0, 3)], x2_send, x2_recv.at[0], sibling
    ).wait_send()
    remote(
        core_sent.at[:, pl.ds(0, 15)], core_held.at[:, pl.ds(0, 15)],
        c_send, c_recv.at[0], sibling,
    ).wait_send()
    for k in range(chunks):
        remote(
            core_held.at[k], core_sib.at[k], cs_send.at[k], cs_recv.at[k], sibling
        ).wait_send()
    for k in range(chunks):
        forward(k).wait_send()
    remote(
        gram.at[pl.ds(0, 15)], gram.at[pl.ds(0, 15)], g1_send, g1_recv.at[0], sibling
    ).wait_send()
    remote(rows_in, rows_in, gz_send, gz_recv.at[0], sibling).wait_send()
    swap.wait_send()
    remote(
        part_in.at[pl.ds(0, 15)], part_in.at[pl.ds(0, 15)], px_send, px_recv, sibling
    ).wait_send()
    remote(
        part_z.at[pl.ds(0, 7)], part_z.at[pl.ds(0, 7)], pz_send, pz_recv, sibling
    ).wait_send()


def write(a, b, c, x, y, z, sem):
    copies = [
        pltpu.make_async_copy(src, dst, sem.at[i])
        for i, (src, dst) in enumerate(((b, y), (a, x), (c, z)))
    ]
    for copy in copies:
        copy.start()
    for copy in copies:
        copy.wait()


def body(snapshots, time_basis):
    f32, bf16 = jnp.float32, jnp.bfloat16
    time_local, load_local, point_local = snapshots.shape
    columns = load_local * 2 * point_local * 8
    rank = time_basis.shape[1]
    k = point_local // LANE
    vmem = pltpu.VMEM
    dma = pltpu.SemaphoreType.DMA
    block = (k, 2, 4, 4, time_local, LANE)
    outs = pl.pallas_call(
        functools.partial(kernel, 1.0 / columns, 1.0 / (rank * point_local * 8)),
        out_shape=(
            jax.ShapeDtypeStruct((32, 512), f32),
            jax.ShapeDtypeStruct((4, 32, point_local), f32),
            jax.ShapeDtypeStruct((32, 64), f32),
        ),
        in_specs=[pl.BlockSpec(memory_space=pl.ANY)] * 2,
        out_specs=(pl.BlockSpec(memory_space=vmem),) * 3,
        scratch_shapes=[
            vmem((rank, 512), f32),
            vmem((k, time_local, load_local, LANE), f32),
            vmem(block, f32),
            vmem(block, f32),
            vmem(block, f32),
            vmem(block, f32),
            vmem((16, 2, 16, 2 * LANE), bf16),
            vmem((16, 2, 16, 2 * LANE), bf16),
            vmem((2, 128, 512), bf16),
            vmem((2, 128, 512), bf16),
            vmem((16, 4, 8, 256), f32),
            vmem((4, 16, 8, 256), f32),
            vmem((4, 8, 256), f32),
            vmem((4, 8, 8, 256), f32),
            vmem((2, 16, 512), f32),
            vmem((k, 16, 8, LANE), f32),
            vmem((k, 16, 8, LANE), f32),
            vmem((k, 16, 8, LANE), f32),
            vmem((2, 128, 128), f32),
            vmem((128, 128), f32),
            vmem((16, LANE), f32),
            vmem((16, 16, LANE), f32),
            vmem((16, LANE), f32),
            vmem((8, 16, LANE), f32),
            pltpu.SemaphoreType.REGULAR((4,)),
            dma, dma((k,)), dma, dma((k, 2)), dma, dma((k,)), dma, dma((k,)), dma((k,)), dma((k,)),
            dma((k,)), dma((k,)), dma, dma((4,)), dma, dma((4,)), dma, dma,
            dma, dma, dma, dma,
        ],
        compiler_params=pltpu.CompilerParams(
            collective_id=0, has_side_effects=True, vmem_limit_bytes=40 * 1024 * 1024
        ),
    )(
        pltpu.with_memory_space_constraint(snapshots, pltpu.HBM),
        pltpu.with_memory_space_constraint(time_basis.T, pltpu.HBM),
    )
    return pl.pallas_call(
        write,
        out_shape=tuple(jax.ShapeDtypeStruct(v.shape, v.dtype) for v in outs),
        in_specs=[pl.BlockSpec(memory_space=vmem)] * 3,
        out_specs=(pl.BlockSpec(memory_space=pl.ANY),) * 3,
        scratch_shapes=[dma((3,))],
        compiler_params=pltpu.CompilerParams(vmem_limit_bytes=4 * 1024 * 1024),
    )(*outs)


def solution(mesh):
    return jax.shard_map(
        body,
        mesh=mesh,
        in_specs=(P("tm", "param", "space"), P()),
        out_specs=(P("tm", None), P("tm", "param", "space"), P("param", None)),
        check_vma=False,
    )
```

```python
import functools

import jax
import jax.numpy as jnp
from jax import lax
from jax.experimental import pallas as pl
from jax.experimental.pallas import tpu as pltpu
from jax.sharding import PartitionSpec as P

MESH = pl.DeviceIdType.MESH
NT = (((1,), (1,)), ((), ()))
NN = (((1,), (0,)), ((), ()))
LANE = 128
ORDER = (
    (1, 0), (0, 1), (3, 0), (0, 3), (1, 1), (3, 3), (1, 3), (3, 1),
    (2, 0), (0, 2), (2, 1), (1, 2), (2, 3), (3, 2), (2, 2),
)


def dot(a, b, dims):
    return lax.dot_general(a, b, dims, preferred_element_type=jnp.float32)


def split(v):
    high = v.astype(jnp.bfloat16)
    return high, (v - high.astype(jnp.float32)).astype(jnp.bfloat16)


def split_3(v):
    high = v.astype(jnp.bfloat16)
    rest = v - high.astype(jnp.float32)
    return (high,) + split(rest)


def kernel(
    scale_time, scale_param,
    x_hbm, basis_hbm, time_out, core_out, param_out,
    basis_ref, staged, sent, mid, held, held_sib, high_buf, low_buf, basis_high, basis_low,
    gram, gram_in, rows_mine, rows_in, tiles,
    core_sent, core_held, core_sib, pair_gram, pair_kept,
    part_mine, part_in, part_sum, part_z,
    relay, basis_sem, load_sem, x1_send, x1_recv, x2_send, x2_recv, c_send, c_recv, cs_send, cs_recv,
    f_send, f_recv, g1_send, g1_recv, gz_send, gz_recv, gy_send, gy_recv,
    px_send, px_recv, pz_send, pz_recv,
):
    sp, tm, me = lax.axis_index("space"), lax.axis_index("tm"), lax.axis_index("param")
    y, x = tm // 4, lax.rem(tm, 4)
    chunks, steps = staged.shape[0], staged.shape[1]

    def peer(dx, dy):
        return lax.rem(y + dy, 4) * 4 + lax.rem(x + dx, 4)

    def along(dz):
        return lax.rem(sp + dz, 8)

    def remote(src, dst, ssem, rsem, target):
        return pltpu.make_async_remote_copy(
            src_ref=src, dst_ref=dst, send_sem=ssem, recv_sem=rsem,
            device_id=target, device_id_type=MESH,
        )

    sibling = (sp, tm, 1 - me)
    ring = (1, 3, 2)
    far = (4, 3, 5, 2, 6, 1, 7)

    def load(k):
        return pltpu.make_async_copy(
            x_hbm.at[:, :, pl.ds(k * LANE, LANE)], staged.at[k], load_sem.at[k]
        )

    barrier = pltpu.get_barrier_semaphore()
    for d in (2, 1, 3):
        pl.semaphore_signal(barrier, inc=1, device_id=(sp, peer(d, 0), me), device_id_type=MESH)
        pl.semaphore_signal(barrier, inc=1, device_id=(sp, peer(0, d), me), device_id_type=MESH)
    for dz in (1, 7):
        pl.semaphore_signal(barrier, inc=1, device_id=(along(dz), tm, me), device_id_type=MESH)
    pl.semaphore_signal(barrier, inc=1, device_id=sibling, device_id_type=MESH)

    for k in range(chunks):
        load(k).start()
    basis_load = pltpu.make_async_copy(basis_hbm, basis_ref, basis_sem)
    basis_load.start()

    for k in range(chunks):
        load(k).wait()
        flat = staged.at[k].reshape(steps * steps, LANE)
        for j in range(16):
            for pp in range(2):
                sent[k, pp, j // 4, j % 4] = flat[pl.ds(2 * j + pp, steps, stride=steps), :]
        if k == 0:
            pl.semaphore_wait(barrier, 9)
        for d in ring:
            tx, ty = lax.rem(x + d, 4), lax.rem(y + d, 4)
            remote(
                sent.at[k, 0, :, tx], mid.at[k, 0, x], x1_send, x1_recv.at[k, 0],
                (sp, y * 4 + tx, me),
            ).start()
            remote(
                sent.at[k, 1, ty], mid.at[k, 1, y], x1_send, x1_recv.at[k, 1],
                (sp, ty * 4 + x, me),
            ).start()
        mid[k, 0, x] = sent[k, 0, :, x]
        mid[k, 1, y] = sent[k, 1, y]

    def pass_on(n):
        for dz in (1, 7):
            pl.semaphore_signal(
                relay.at[n], inc=1, device_id=(along(dz), tm, me), device_id_type=MESH
            )

    row = lax.broadcasted_iota(jnp.int32, (128, 64), 0)
    col = lax.broadcasted_iota(jnp.int32, (128, 64), 1)
    basis_load.wait()
    parts = split(basis_ref[...])
    for pp in range(2):
        pick = jnp.where(
            (lax.rem(row, 8) // 4 == pp) & (col == (row // 8) * 4 + lax.rem(row, 4)), 1.0, 0.0
        ).astype(jnp.bfloat16)
        basis_high[pp] = dot(pick, parts[0], NN).astype(jnp.bfloat16)
        basis_low[pp] = dot(pick, parts[1], NN).astype(jnp.bfloat16)

    gram[...] = jnp.zeros_like(gram)
    pair_gram[...] = jnp.zeros_like(pair_gram)

    for k in range(chunks):
        for pp in range(2):
            remote(
                sent.at[k, pp, pl.ds(0, 3)], mid.at[k, pp, pl.ds(0, 3)],
                x1_send, x1_recv.at[k, pp], sibling,
            ).wait_recv()
        for d in ring:
            tx, ty = lax.rem(x + d, 4), lax.rem(y + d, 4)
            remote(
                mid.at[k, 0, :, ty], held.at[k, 0, y], x2_send, x2_recv.at[k],
                (sp, ty * 4 + x, me),
            ).start()
            remote(
                mid.at[k, 1, :, tx], held.at[k, 1, :, x], x2_send, x2_recv.at[k],
                (sp, y * 4 + tx, me),
            ).start()
        held[k, 0, y] = mid[k, 0, :, y]
        held[k, 1, :, x] = mid[k, 1, :, x]

    def core_back(k):
        remote(
            core_sent.at[k, pl.ds(0, 15)], core_held.at[k, pl.ds(0, 15)],
            c_send, c_recv.at[k], sibling,
        ).wait_recv()
        remote(
            core_held.at[k], core_sib.at[k], cs_send.at[k], cs_recv.at[k], sibling
        ).start()

    def core_write(k):
        flat = core_held.at[k].reshape(128, LANE)
        for r in range(4):
            core_out[r, :, k * LANE:(k + 1) * LANE] = flat[pl.ds(r, 32, stride=4), :]

    def core_pair(k):
        remote(
            core_held.at[k], core_sib.at[k], cs_send.at[k], cs_recv.at[k], sibling
        ).wait_recv()
        high, low = split(core_held[k].reshape(128, LANE))
        high_2, low_2 = split(core_sib[k].reshape(128, LANE))
        pair_gram[0] += (dot(high, low, NT) + dot(low, high, NT)) + dot(high, high, NT)
        pair_gram[1] += (dot(high, low_2, NT) + dot(low, high_2, NT)) + dot(high, high_2, NT)

    def forward(k):
        return remote(held.at[k], held_sib.at[k], f_send.at[k], f_recv.at[k], sibling)

    def convert(blocks, k):
        for pp in range(2):
            high, low = split(blocks[k, pp].reshape(16, 2, 16, LANE))
            high_buf[:, :, :, pp * LANE:(pp + 1) * LANE] = high
            low_buf[:, :, :, pp * LANE:(pp + 1) * LANE] = low

    def add_gram():
        all_high = high_buf[...].reshape(512, 2 * LANE)
        all_low = low_buf[...].reshape(512, 2 * LANE)
        high = high_buf[:, me].reshape(256, 2 * LANE)
        low = low_buf[:, me].reshape(256, 2 * LANE)
        add = (dot(high, all_low, NT) + dot(low, all_high, NT)) + dot(high, all_high, NT)
        add = add.reshape(16, 2, 8, 512)
        gram[:, 0:2] += add[:, :, :, :256]
        gram[:, 2:4] += add[:, :, :, 256:]

    for k in range(chunks):
        remote(
            mid.at[k, :, pl.ds(0, 3)], held.at[k, :, pl.ds(0, 3)],
            x2_send, x2_recv.at[k], sibling,
        ).wait_recv()
        forward(k).start()
        convert(held, k)
        total = None
        for pp in range(2):
            high = high_buf[:, :, :, pp * LANE:(pp + 1) * LANE].reshape(512, LANE)
            low = low_buf[:, :, :, pp * LANE:(pp + 1) * LANE].reshape(512, LANE)
            term = (
                dot(basis_high[pp], low, NN) + dot(basis_low[pp], high, NN)
            ) + dot(basis_high[pp], high, NN)
            total = term if total is None else total + term
        core_sent[k] = total.reshape(16, 8, LANE)
        if 1 <= k <= 4:
            pl.semaphore_wait(relay.at[k - 1], 2)
        if k <= 3:
            pass_on(k)
        core_held[k, tm] = core_sent[k, tm]
        for dx, dy in ORDER[::-1]:
            to = peer(dx, dy)
            remote(
                core_sent.at[k, to], core_held.at[k, tm], c_send, c_recv.at[k], (sp, to, me)
            ).start()
        add_gram()
        forward(k).wait_recv()
        convert(held_sib, k)
        add_gram()

    for h in range(4):
        for dx, dy in ORDER[::-1]:
            to = peer(dx, dy)
            remote(
                gram.at[to, h], gram_in.at[h, tm], g1_send, g1_recv.at[h], (sp, to, me)
            ).start()
        gram_in[h, tm] = gram[tm, h]

    def spread(h):
        remote(
            gram.at[pl.ds(0, 15), h], gram_in.at[h, pl.ds(0, 15)],
            g1_send, g1_recv.at[h], sibling,
        ).wait_recv()
        rows = gram_in[h, 0]
        for j in range(1, 16):
            rows = rows + gram_in[h, j]
        rows_mine[h] = rows
        for dz in far + (0,):
            remote(
                rows_mine.at[h], rows_in.at[h, sp], gz_send, gz_recv.at[h],
                (along(dz), tm, 1 - me),
            ).start()

    for k in range(0, chunks - 1):
        core_back(k)
    for k in range(0, chunks - 2):
        core_pair(k)
    for h in range(0, 1):
        spread(h)
    for k in range(chunks - 1, chunks):
        core_back(k)
    for k in range(chunks - 2, chunks):
        core_pair(k)
    for h in range(1, 2):
        spread(h)
    row = lax.broadcasted_iota(jnp.int32, (128, 128), 0)
    col = lax.broadcasted_iota(jnp.int32, (128, 128), 1)
    same = lax.rem(row, 4) == lax.rem(col, 4)
    row = lax.broadcasted_iota(jnp.int32, (64, 128), 0)
    col = lax.broadcasted_iota(jnp.int32, (64, 128), 1)
    part = jnp.zeros((32, 64), jnp.float32)
    for other in range(2):
        at = (1 - me) if other else me
        place = jnp.where(row == at * 32 + col // 4, 1.0, 0.0).astype(jnp.bfloat16)
        pair_kept[...] = jnp.where(same, pair_gram[other], 0.0)
        summed = (
            (pair_kept[pl.ds(0, 32, stride=4), :] + pair_kept[pl.ds(1, 32, stride=4), :])
            + (pair_kept[pl.ds(2, 32, stride=4), :] + pair_kept[pl.ds(3, 32, stride=4), :])
        )
        for small in split_3(summed):
            part = part + dot(small, place, NT)
    part_mine[...] = jnp.concatenate([part[:16], part[16:]], axis=1)
    for dx, dy in ORDER[::-1]:
        remote(
            part_mine, part_in.at[tm], px_send, px_recv, (sp, peer(dx, dy), me)
        ).start()
    part_in[tm] = part_mine[...]

    for h in range(2, 4):
        spread(h)

    remote(
        part_in.at[pl.ds(0, 15)], part_in.at[pl.ds(0, 15)], px_send, px_recv, sibling
    ).wait_recv()
    part = part_in[0]
    for j in range(1, 16):
        part = part + part_in[j]
    part_sum[...] = part
    for dz in far:
        to = along(dz)
        remote(part_sum, part_z.at[sp], pz_send, pz_recv, (to, tm, me)).start()
    part_z[sp] = part

    for k in range(chunks):
        core_write(k)

    for h in range(4):
        remote(
            gram_in.at[h, pl.ds(0, 8)], rows_in.at[h], gz_send, gz_recv.at[h], sibling
        ).wait_recv()
        rows = rows_in[h, 0]
        for j in range(1, 8):
            rows = rows + rows_in[h, j]
        tiles[1 - me, (h % 2) * 8:(h % 2) * 8 + 8, (h // 2) * 256:(h // 2) * 256 + 256] = rows * scale_time
    swap = remote(tiles.at[1 - me], tiles.at[1 - me], gy_send, gy_recv, sibling)
    swap.start()

    remote(
        part_z.at[pl.ds(0, 7)], part_z.at[pl.ds(0, 7)], pz_send, pz_recv, sibling
    ).wait_recv()
    part = part_z[0]
    for j in range(1, 8):
        part = part + part_z[j]
    part = part * scale_param
    param_out[0:16, :] = part[:, :64]
    param_out[16:32, :] = part[:, 64:]

    swap.wait_recv()
    time_out[0:16, :] = tiles[0]
    time_out[16:32, :] = tiles[1]

    remote(
        sent.at[:, :, pl.ds(0, 3)], mid.at[:, :, pl.ds(0, 3)], x1_send, x1_recv.at[0, 0], sibling
    ).wait_send()
    remote(
        mid.at[:, :, pl.ds(0, 3)], held.at[:, :, pl.ds(0, 3)], x2_send, x2_recv.at[0], sibling
    ).wait_send()
    remote(
        core_sent.at[:, pl.ds(0, 15)], core_held.at[:, pl.ds(0, 15)],
        c_send, c_recv.at[0], sibling,
    ).wait_send()
    for k in range(chunks):
        remote(
            core_held.at[k], core_sib.at[k], cs_send.at[k], cs_recv.at[k], sibling
        ).wait_send()
    for k in range(chunks):
        forward(k).wait_send()
    remote(
        gram.at[pl.ds(0, 15)], gram.at[pl.ds(0, 15)], g1_send, g1_recv.at[0], sibling
    ).wait_send()
    remote(rows_in, rows_in, gz_send, gz_recv.at[0], sibling).wait_send()
    swap.wait_send()
    remote(
        part_in.at[pl.ds(0, 15)], part_in.at[pl.ds(0, 15)], px_send, px_recv, sibling
    ).wait_send()
    remote(
        part_z.at[pl.ds(0, 7)], part_z.at[pl.ds(0, 7)], pz_send, pz_recv, sibling
    ).wait_send()


def write(a, b, c, x, y, z, sem):
    copies = [
        pltpu.make_async_copy(src, dst, sem.at[i])
        for i, (src, dst) in enumerate(((b, y), (a, x), (c, z)))
    ]
    for copy in copies:
        copy.start()
    for copy in copies:
        copy.wait()


def body(snapshots, time_basis):
    f32, bf16 = jnp.float32, jnp.bfloat16
    time_local, load_local, point_local = snapshots.shape
    columns = load_local * 2 * point_local * 8
    rank = time_basis.shape[1]
    k = point_local // LANE
    vmem = pltpu.VMEM
    dma = pltpu.SemaphoreType.DMA
    block = (k, 2, 4, 4, time_local, LANE)
    outs = pl.pallas_call(
        functools.partial(kernel, 1.0 / columns, 1.0 / (rank * point_local * 8)),
        out_shape=(
            jax.ShapeDtypeStruct((32, 512), f32),
            jax.ShapeDtypeStruct((4, 32, point_local), f32),
            jax.ShapeDtypeStruct((32, 64), f32),
        ),
        in_specs=[pl.BlockSpec(memory_space=pl.ANY)] * 2,
        out_specs=(pl.BlockSpec(memory_space=vmem),) * 3,
        scratch_shapes=[
            vmem((rank, 512), f32),
            vmem((k, time_local, load_local, LANE), f32),
            vmem(block, f32),
            vmem(block, f32),
            vmem(block, f32),
            vmem(block, f32),
            vmem((16, 2, 16, 2 * LANE), bf16),
            vmem((16, 2, 16, 2 * LANE), bf16),
            vmem((2, 128, 512), bf16),
            vmem((2, 128, 512), bf16),
            vmem((16, 4, 8, 256), f32),
            vmem((4, 16, 8, 256), f32),
            vmem((4, 8, 256), f32),
            vmem((4, 8, 8, 256), f32),
            vmem((2, 16, 512), f32),
            vmem((k, 16, 8, LANE), f32),
            vmem((k, 16, 8, LANE), f32),
            vmem((k, 16, 8, LANE), f32),
            vmem((2, 128, 128), f32),
            vmem((128, 128), f32),
            vmem((16, LANE), f32),
            vmem((16, 16, LANE), f32),
            vmem((16, LANE), f32),
            vmem((8, 16, LANE), f32),
            pltpu.SemaphoreType.REGULAR((4,)),
            dma, dma((k,)), dma, dma((k, 2)), dma, dma((k,)), dma, dma((k,)), dma((k,)), dma((k,)),
            dma((k,)), dma((k,)), dma, dma((4,)), dma, dma((4,)), dma, dma,
            dma, dma, dma, dma,
        ],
        compiler_params=pltpu.CompilerParams(
            collective_id=0, has_side_effects=True, vmem_limit_bytes=40 * 1024 * 1024
        ),
    )(
        pltpu.with_memory_space_constraint(snapshots, pltpu.HBM),
        pltpu.with_memory_space_constraint(time_basis.T, pltpu.HBM),
    )
    return pl.pallas_call(
        write,
        out_shape=tuple(jax.ShapeDtypeStruct(v.shape, v.dtype) for v in outs),
        in_specs=[pl.BlockSpec(memory_space=vmem)] * 3,
        out_specs=(pl.BlockSpec(memory_space=pl.ANY),) * 3,
        scratch_shapes=[dma((3,))],
        compiler_params=pltpu.CompilerParams(vmem_limit_bytes=4 * 1024 * 1024),
    )(*outs)


def solution(mesh):
    return jax.shard_map(
        body,
        mesh=mesh,
        in_specs=(P("tm", "param", "space"), P()),
        out_specs=(P("tm", None), P("tm", "param", "space"), P("param", None)),
        check_vma=False,
    )
```

```python
import functools

import jax
import jax.numpy as jnp
from jax import lax
from jax.experimental import pallas as pl
from jax.experimental.pallas import tpu as pltpu
from jax.sharding import PartitionSpec as P

MESH = pl.DeviceIdType.MESH
NT = (((1,), (1,)), ((), ()))
NN = (((1,), (0,)), ((), ()))
LANE = 128
ORDER = (
    (1, 0), (0, 1), (3, 0), (0, 3), (1, 1), (3, 3), (1, 3), (3, 1),
    (2, 0), (0, 2), (2, 1), (1, 2), (2, 3), (3, 2), (2, 2),
)


def dot(a, b, dims):
    return lax.dot_general(a, b, dims, preferred_element_type=jnp.float32)


def split(v):
    high = v.astype(jnp.bfloat16)
    return high, (v - high.astype(jnp.float32)).astype(jnp.bfloat16)


def split_3(v):
    high = v.astype(jnp.bfloat16)
    rest = v - high.astype(jnp.float32)
    return (high,) + split(rest)


def kernel(
    scale_time, scale_param,
    x_hbm, basis_hbm, time_out, core_out, param_out,
    basis_ref, staged, sent, mid, held, held_sib, high_buf, low_buf, basis_high, basis_low,
    gram, gram_in, rows_mine, rows_in, tiles,
    core_sent, core_held, core_sib, pair_gram, pair_kept,
    part_mine, part_in, part_sum, part_z,
    relay, basis_sem, load_sem, x1_send, x1_recv, x2_send, x2_recv, c_send, c_recv, cs_send, cs_recv,
    f_send, f_recv, g1_send, g1_recv, gz_send, gz_recv, gy_send, gy_recv,
    px_send, px_recv, pz_send, pz_recv,
):
    sp, tm, me = lax.axis_index("space"), lax.axis_index("tm"), lax.axis_index("param")
    y, x = tm // 4, lax.rem(tm, 4)
    chunks, steps = staged.shape[0], staged.shape[1]

    def peer(dx, dy):
        return lax.rem(y + dy, 4) * 4 + lax.rem(x + dx, 4)

    def along(dz):
        return lax.rem(sp + dz, 8)

    def remote(src, dst, ssem, rsem, target):
        return pltpu.make_async_remote_copy(
            src_ref=src, dst_ref=dst, send_sem=ssem, recv_sem=rsem,
            device_id=target, device_id_type=MESH,
        )

    sibling = (sp, tm, 1 - me)
    ring = (2, 1, 3)
    far = (4, 3, 5, 2, 6, 1, 7)

    def load(k):
        return pltpu.make_async_copy(
            x_hbm.at[:, :, pl.ds(k * LANE, LANE)], staged.at[k], load_sem.at[k]
        )

    barrier = pltpu.get_barrier_semaphore()
    for d in (2, 1, 3):
        pl.semaphore_signal(barrier, inc=1, device_id=(sp, peer(d, 0), me), device_id_type=MESH)
        pl.semaphore_signal(barrier, inc=1, device_id=(sp, peer(0, d), me), device_id_type=MESH)
    for dz in (1, 7):
        pl.semaphore_signal(barrier, inc=1, device_id=(along(dz), tm, me), device_id_type=MESH)
    pl.semaphore_signal(barrier, inc=1, device_id=sibling, device_id_type=MESH)

    for k in range(chunks):
        load(k).start()
    basis_load = pltpu.make_async_copy(basis_hbm, basis_ref, basis_sem)
    basis_load.start()

    for k in range(chunks):
        load(k).wait()
        flat = staged.at[k].reshape(steps * steps, LANE)
        for j in range(16):
            for pp in range(2):
                sent[k, pp, j // 4, j % 4] = flat[pl.ds(2 * j + pp, steps, stride=steps), :]
        if k == 0:
            pl.semaphore_wait(barrier, 9)
        for d in ring:
            tx, ty = lax.rem(x + d, 4), lax.rem(y + d, 4)
            remote(
                sent.at[k, 0, :, tx], mid.at[k, 0, x], x1_send, x1_recv.at[k, 0],
                (sp, y * 4 + tx, me),
            ).start()
            remote(
                sent.at[k, 1, ty], mid.at[k, 1, y], x1_send, x1_recv.at[k, 1],
                (sp, ty * 4 + x, me),
            ).start()
        mid[k, 0, x] = sent[k, 0, :, x]
        mid[k, 1, y] = sent[k, 1, y]

    def pass_on(n):
        for dz in (1, 7):
            pl.semaphore_signal(
                relay.at[n], inc=1, device_id=(along(dz), tm, me), device_id_type=MESH
            )

    row = lax.broadcasted_iota(jnp.int32, (128, 64), 0)
    col = lax.broadcasted_iota(jnp.int32, (128, 64), 1)
    basis_load.wait()
    parts = split(basis_ref[...])
    for pp in range(2):
        pick = jnp.where(
            (lax.rem(row, 8) // 4 == pp) & (col == (row // 8) * 4 + lax.rem(row, 4)), 1.0, 0.0
        ).astype(jnp.bfloat16)
        basis_high[pp] = dot(pick, parts[0], NN).astype(jnp.bfloat16)
        basis_low[pp] = dot(pick, parts[1], NN).astype(jnp.bfloat16)

    gram[...] = jnp.zeros_like(gram)
    pair_gram[...] = jnp.zeros_like(pair_gram)

    for k in range(chunks):
        for pp in range(2):
            remote(
                sent.at[k, pp, pl.ds(0, 3)], mid.at[k, pp, pl.ds(0, 3)],
                x1_send, x1_recv.at[k, pp], sibling,
            ).wait_recv()
        for d in ring:
            tx, ty = lax.rem(x + d, 4), lax.rem(y + d, 4)
            remote(
                mid.at[k, 0, :, ty], held.at[k, 0, y], x2_send, x2_recv.at[k],
                (sp, ty * 4 + x, me),
            ).start()
            remote(
                mid.at[k, 1, :, tx], held.at[k, 1, :, x], x2_send, x2_recv.at[k],
                (sp, y * 4 + tx, me),
            ).start()
        held[k, 0, y] = mid[k, 0, :, y]
        held[k, 1, :, x] = mid[k, 1, :, x]

    def core_back(k):
        remote(
            core_sent.at[k, pl.ds(0, 15)], core_held.at[k, pl.ds(0, 15)],
            c_send, c_recv.at[k], sibling,
        ).wait_recv()
        remote(
            core_held.at[k], core_sib.at[k], cs_send.at[k], cs_recv.at[k], sibling
        ).start()

    def core_write(k):
        flat = core_held.at[k].reshape(128, LANE)
        for r in range(4):
            core_out[r, :, k * LANE:(k + 1) * LANE] = flat[pl.ds(r, 32, stride=4), :]

    def core_pair(k):
        remote(
            core_held.at[k], core_sib.at[k], cs_send.at[k], cs_recv.at[k], sibling
        ).wait_recv()
        high, low = split(core_held[k].reshape(128, LANE))
        high_2, low_2 = split(core_sib[k].reshape(128, LANE))
        pair_gram[0] += (dot(high, low, NT) + dot(low, high, NT)) + dot(high, high, NT)
        pair_gram[1] += (dot(high, low_2, NT) + dot(low, high_2, NT)) + dot(high, high_2, NT)

    def forward(k):
        return remote(held.at[k], held_sib.at[k], f_send.at[k], f_recv.at[k], sibling)

    def convert(blocks, k):
        for pp in range(2):
            high, low = split(blocks[k, pp].reshape(16, 2, 16, LANE))
            high_buf[:, :, :, pp * LANE:(pp + 1) * LANE] = high
            low_buf[:, :, :, pp * LANE:(pp + 1) * LANE] = low

    def add_gram():
        all_high = high_buf[...].reshape(512, 2 * LANE)
        all_low = low_buf[...].reshape(512, 2 * LANE)
        high = high_buf[:, me].reshape(256, 2 * LANE)
        low = low_buf[:, me].reshape(256, 2 * LANE)
        add = (dot(high, all_low, NT) + dot(low, all_high, NT)) + dot(high, all_high, NT)
        add = add.reshape(16, 2, 8, 512)
        gram[:, 0:2] += add[:, :, :, :256]
        gram[:, 2:4] += add[:, :, :, 256:]

    for k in range(chunks):
        remote(
            mid.at[k, :, pl.ds(0, 3)], held.at[k, :, pl.ds(0, 3)],
            x2_send, x2_recv.at[k], sibling,
        ).wait_recv()
        forward(k).start()
        convert(held, k)
        total = None
        for pp in range(2):
            high = high_buf[:, :, :, pp * LANE:(pp + 1) * LANE].reshape(512, LANE)
            low = low_buf[:, :, :, pp * LANE:(pp + 1) * LANE].reshape(512, LANE)
            term = (
                dot(basis_high[pp], low, NN) + dot(basis_low[pp], high, NN)
            ) + dot(basis_high[pp], high, NN)
            total = term if total is None else total + term
        core_sent[k] = total.reshape(16, 8, LANE)
        if 1 <= k <= 4:
            pl.semaphore_wait(relay.at[k - 1], 2)
        if k <= 3:
            pass_on(k)
        core_held[k, tm] = core_sent[k, tm]
        for dx, dy in ORDER[::-1]:
            to = peer(dx, dy)
            remote(
                core_sent.at[k, to], core_held.at[k, tm], c_send, c_recv.at[k], (sp, to, me)
            ).start()
        add_gram()
        forward(k).wait_recv()
        convert(held_sib, k)
        add_gram()

    for h in range(4):
        for dx, dy in ORDER[::-1]:
            to = peer(dx, dy)
            remote(
                gram.at[to, h], gram_in.at[h, tm], g1_send, g1_recv.at[h], (sp, to, me)
            ).start()
        gram_in[h, tm] = gram[tm, h]

    def spread(h):
        remote(
            gram.at[pl.ds(0, 15), h], gram_in.at[h, pl.ds(0, 15)],
            g1_send, g1_recv.at[h], sibling,
        ).wait_recv()
        rows = gram_in[h, 0]
        for j in range(1, 16):
            rows = rows + gram_in[h, j]
        rows_mine[h] = rows
        for dz in far + (0,):
            remote(
                rows_mine.at[h], rows_in.at[h, sp], gz_send, gz_recv.at[h],
                (along(dz), tm, 1 - me),
            ).start()

    for k in range(0, chunks - 1):
        core_back(k)
    for k in range(0, chunks - 2):
        core_pair(k)
    for h in range(0, 1):
        spread(h)
    for k in range(chunks - 1, chunks):
        core_back(k)
    for k in range(chunks - 2, chunks):
        core_pair(k)
    for h in range(1, 2):
        spread(h)
    row = lax.broadcasted_iota(jnp.int32, (128, 128), 0)
    col = lax.broadcasted_iota(jnp.int32, (128, 128), 1)
    same = lax.rem(row, 4) == lax.rem(col, 4)
    row = lax.broadcasted_iota(jnp.int32, (64, 128), 0)
    col = lax.broadcasted_iota(jnp.int32, (64, 128), 1)
    part = jnp.zeros((32, 64), jnp.float32)
    for other in range(2):
        at = (1 - me) if other else me
        place = jnp.where(row == at * 32 + col // 4, 1.0, 0.0).astype(jnp.bfloat16)
        pair_kept[...] = jnp.where(same, pair_gram[other], 0.0)
        summed = (
            (pair_kept[pl.ds(0, 32, stride=4), :] + pair_kept[pl.ds(1, 32, stride=4), :])
            + (pair_kept[pl.ds(2, 32, stride=4), :] + pair_kept[pl.ds(3, 32, stride=4), :])
        )
        for small in split_3(summed):
            part = part + dot(small, place, NT)
    part_mine[...] = jnp.concatenate([part[:16], part[16:]], axis=1)
    for dx, dy in ORDER[::-1]:
        remote(
            part_mine, part_in.at[tm], px_send, px_recv, (sp, peer(dx, dy), me)
        ).start()
    part_in[tm] = part_mine[...]

    for h in range(2, 4):
        spread(h)

    remote(
        part_in.at[pl.ds(0, 15)], part_in.at[pl.ds(0, 15)], px_send, px_recv, sibling
    ).wait_recv()
    part = part_in[0]
    for j in range(1, 16):
        part = part + part_in[j]
    part_sum[...] = part
    for dz in far:
        to = along(dz)
        remote(part_sum, part_z.at[sp], pz_send, pz_recv, (to, tm, me)).start()
    part_z[sp] = part

    for k in range(chunks):
        core_write(k)

    for h in range(4):
        remote(
            gram_in.at[h, pl.ds(0, 8)], rows_in.at[h], gz_send, gz_recv.at[h], sibling
        ).wait_recv()
        rows = rows_in[h, 0]
        for j in range(1, 8):
            rows = rows + rows_in[h, j]
        tiles[1 - me, (h % 2) * 8:(h % 2) * 8 + 8, (h // 2) * 256:(h // 2) * 256 + 256] = rows * scale_time
    swap = remote(tiles.at[1 - me], tiles.at[1 - me], gy_send, gy_recv, sibling)
    swap.start()

    remote(
        part_z.at[pl.ds(0, 7)], part_z.at[pl.ds(0, 7)], pz_send, pz_recv, sibling
    ).wait_recv()
    part = part_z[0]
    for j in range(1, 8):
        part = part + part_z[j]
    part = part * scale_param
    param_out[0:16, :] = part[:, :64]
    param_out[16:32, :] = part[:, 64:]

    swap.wait_recv()
    time_out[0:16, :] = tiles[0]
    time_out[16:32, :] = tiles[1]

    remote(
        sent.at[:, :, pl.ds(0, 3)], mid.at[:, :, pl.ds(0, 3)], x1_send, x1_recv.at[0, 0], sibling
    ).wait_send()
    remote(
        mid.at[:, :, pl.ds(0, 3)], held.at[:, :, pl.ds(0, 3)], x2_send, x2_recv.at[0], sibling
    ).wait_send()
    remote(
        core_sent.at[:, pl.ds(0, 15)], core_held.at[:, pl.ds(0, 15)],
        c_send, c_recv.at[0], sibling,
    ).wait_send()
    for k in range(chunks):
        remote(
            core_held.at[k], core_sib.at[k], cs_send.at[k], cs_recv.at[k], sibling
        ).wait_send()
    for k in range(chunks):
        forward(k).wait_send()
    remote(
        gram.at[pl.ds(0, 15)], gram.at[pl.ds(0, 15)], g1_send, g1_recv.at[0], sibling
    ).wait_send()
    remote(rows_in, rows_in, gz_send, gz_recv.at[0], sibling).wait_send()
    swap.wait_send()
    remote(
        part_in.at[pl.ds(0, 15)], part_in.at[pl.ds(0, 15)], px_send, px_recv, sibling
    ).wait_send()
    remote(
        part_z.at[pl.ds(0, 7)], part_z.at[pl.ds(0, 7)], pz_send, pz_recv, sibling
    ).wait_send()


def write(a, b, c, x, y, z, sem):
    copies = [
        pltpu.make_async_copy(src, dst, sem.at[i])
        for i, (src, dst) in enumerate(((b, y), (a, x), (c, z)))
    ]
    for copy in copies:
        copy.start()
    for copy in copies:
        copy.wait()


def body(snapshots, time_basis):
    f32, bf16 = jnp.float32, jnp.bfloat16
    time_local, load_local, point_local = snapshots.shape
    columns = load_local * 2 * point_local * 8
    rank = time_basis.shape[1]
    k = point_local // LANE
    vmem = pltpu.VMEM
    dma = pltpu.SemaphoreType.DMA
    block = (k, 2, 4, 4, time_local, LANE)
    outs = pl.pallas_call(
        functools.partial(kernel, 1.0 / columns, 1.0 / (rank * point_local * 8)),
        out_shape=(
            jax.ShapeDtypeStruct((32, 512), f32),
            jax.ShapeDtypeStruct((4, 32, point_local), f32),
            jax.ShapeDtypeStruct((32, 64), f32),
        ),
        in_specs=[pl.BlockSpec(memory_space=pl.ANY)] * 2,
        out_specs=(pl.BlockSpec(memory_space=vmem),) * 3,
        scratch_shapes=[
            vmem((rank, 512), f32),
            vmem((k, time_local, load_local, LANE), f32),
            vmem(block, f32),
            vmem(block, f32),
            vmem(block, f32),
            vmem(block, f32),
            vmem((16, 2, 16, 2 * LANE), bf16),
            vmem((16, 2, 16, 2 * LANE), bf16),
            vmem((2, 128, 512), bf16),
            vmem((2, 128, 512), bf16),
            vmem((16, 4, 8, 256), f32),
            vmem((4, 16, 8, 256), f32),
            vmem((4, 8, 256), f32),
            vmem((4, 8, 8, 256), f32),
            vmem((2, 16, 512), f32),
            vmem((k, 16, 8, LANE), f32),
            vmem((k, 16, 8, LANE), f32),
            vmem((k, 16, 8, LANE), f32),
            vmem((2, 128, 128), f32),
            vmem((128, 128), f32),
            vmem((16, LANE), f32),
            vmem((16, 16, LANE), f32),
            vmem((16, LANE), f32),
            vmem((8, 16, LANE), f32),
            pltpu.SemaphoreType.REGULAR((4,)),
            dma, dma((k,)), dma, dma((k, 2)), dma, dma((k,)), dma, dma((k,)), dma((k,)), dma((k,)),
            dma((k,)), dma((k,)), dma, dma((4,)), dma, dma((4,)), dma, dma,
            dma, dma, dma, dma,
        ],
        compiler_params=pltpu.CompilerParams(
            collective_id=0, has_side_effects=True, vmem_limit_bytes=40 * 1024 * 1024
        ),
    )(
        pltpu.with_memory_space_constraint(snapshots, pltpu.HBM),
        pltpu.with_memory_space_constraint(time_basis.T, pltpu.HBM),
    )
    return pl.pallas_call(
        write,
        out_shape=tuple(jax.ShapeDtypeStruct(v.shape, v.dtype) for v in outs),
        in_specs=[pl.BlockSpec(memory_space=vmem)] * 3,
        out_specs=(pl.BlockSpec(memory_space=pl.ANY),) * 3,
        scratch_shapes=[dma((3,))],
        compiler_params=pltpu.CompilerParams(vmem_limit_bytes=4 * 1024 * 1024),
    )(*outs)


def solution(mesh):
    return jax.shard_map(
        body,
        mesh=mesh,
        in_specs=(P("tm", "param", "space"), P()),
        out_specs=(P("tm", None), P("tm", "param", "space"), P("param", None)),
        check_vma=False,
    )
```
